32 devices in a mesh: dp: 8 (over z, y), tensor: 4 (over x, core).
Axes of the slice: x: 2, y: 2, z: 4, core: 2. Of those that a mesh axis runs over, the one named last changes fastest.
Arguments:
- inputs: bfloat16 [25088, 512], P(('dp', 'tensor')), may hold values from -6 to 6
- image_count: int32 [8], P('dp'), may hold values from 15 to 16, as said below
- rel_index: int32 [49, 49], replicated, may hold values from 0 to 168, as said below
- rel_table: float32 [169, 16], P(None, 'tensor'), may hold values from -8 to 400
- norm1_gain: float32 [512], replicated, may hold values from 0.5 to 1.5
- norm1_shift: float32 [512], replicated, may hold values from -3 to 3
- w_qkv: bfloat16 [3, 512, 512], P(None, None, 'tensor'), may hold values from -0.25 to 0.25
- bias_qv: float32 [2, 512], P(None, 'tensor'), may hold values from -3 to 3
- w_proj: bfloat16 [512, 512], P('tensor'), may hold values from -0.625 to 0.625
- b_proj: float32 [512], replicated, may hold values from -2 to 2
- norm2_gain: float32 [512], replicated, may hold values from 0.5 to 1.5
- norm2_shift: float32 [512], replicated, may hold values from -3 to 3
- w_fc1: bfloat16 [512, 2048], P(None, 'tensor'), may hold values from -0.25 to 0.25
- b_fc1: float32 [2048], P('tensor'), may hold values from -3 to 3
- w_fc2: bfloat16 [2048, 512], P('tensor'), may hold values from -0.1875 to 0.1875
- b_fc2: float32 [512], replicated, may hold values from -2 to 2
- out_grad: bfloat16 [25088, 512], P(('dp', 'tensor')), may hold values from -6 to 6
Outputs:
- outputs: bfloat16 [25088, 512], P(('dp', 'tensor'))
- in_grad: bfloat16 [25088, 512], P(('dp', 'tensor'))
- g_table: float32 [169, 16], P(None, 'tensor')
- g_norm1_gain: float32 [512], replicated
- g_norm1_shift: float32 [512], replicated
- g_qkv: float32 [3, 512, 512], P(None, None, 'tensor')
- g_bias_qv: float32 [2, 512], P(None, 'tensor')
- g_proj: float32 [512, 512], P('tensor')
- g_b_proj: float32 [512], replicated
- g_norm2_gain: float32 [512], replicated
- g_norm2_shift: float32 [512], replicated
- g_fc1: float32 [512, 2048], P(None, 'tensor')
- g_b_fc1: float32 [2048], P('tensor')
- g_fc2: float32 [2048, 512], P('tensor')
- g_b_fc2: float32 [512], replicated
The draws below stay inside these ranges and needn't reach their ends.
Inputs may be any that keep to these rules, and one draw needn't show every extreme that they name: `image_count`: each value is 15 or 16; both occur in every draw. `rel_index`: entries for equal offsets between query and key position are equal, unequal offsets give unequal entries.
All inputs are finite; a program needn't handle non-finite values.
Results may differ from the reference program's by a relative error of at most 0.015.
Values may be sent and summed in bfloat16 or wider, within the bound.
No kernel may reach another device: no remote copies, remote signals or barrier semaphores. Data moves between devices by JAX's collectives and lax.ppermute only.
A program may use at most 128 MiB of HBM per device.

```python
import jax
import jax.numpy as jnp
from jax import lax

D = 512
HEADS = 16
HEAD_DIM = 32
FF = 2048
WIN_SIDE = 7
IMG_DEV = 16
WINDOW = 49
OFFSETS = 169
IMG_TOKENS = 196
TOKENS = 25088
N_DP = 8


def draw_image_count(key, part):
    n_groups = N_DP
    base = IMG_DEV - jax.random.randint(jax.random.fold_in(key, 1), (n_groups,), 0, 2)
    order = jax.random.permutation(jax.random.fold_in(key, 2), n_groups)
    base = base.at[order[0]].set(IMG_DEV)
    base = base.at[order[1]].set(IMG_DEV - 1)
    return base.astype(jnp.int32)


def draw_rel_index(key, part):
    span = 2 * WIN_SIDE - 1
    pos = jnp.arange(WINDOW, dtype=jnp.int32)
    row = pos // WIN_SIDE
    col = pos % WIN_SIDE
    offset = (row[:, None] - row[None, :] + WIN_SIDE - 1) * span + (col[:, None] - col[None, :] + WIN_SIDE - 1)
    relabel = jax.random.permutation(jax.random.fold_in(key, 3), OFFSETS).astype(jnp.int32)
    return relabel[offset].astype(jnp.int32)


def draw_rel_table(key, part):
    base = jax.random.normal(jax.random.fold_in(key, 4), (OFFSETS, HEADS), jnp.float32)
    return jnp.clip(base, -8.0, 400.0).astype(jnp.float32)


def levels(rng, shape, split, smallest, largest):
    def one(axis_at, blocks):
        draws = jax.random.uniform(jax.random.fold_in(jax.random.fold_in(rng, 6), axis_at), (blocks,), jnp.float32, smallest / len(split), largest / len(split))
        return jnp.repeat(jnp.exp(draws), shape[axis_at] // blocks).reshape((-1,) + (1,) * (len(shape) - axis_at - 1))

    factor_of = one(*split[0])
    for cut in split[1:]:
        factor_of = factor_of * one(*cut)
    return factor_of


def gaussian(rng, shape, spread, reach, shards=(), held_as=jnp.bfloat16):
    entries = jax.random.normal(rng, shape, jnp.float32) * spread
    if len(shards) > 0:
        entries = levels(rng, shape, shards, -0.22, 0.18) * entries
    return jnp.clip(entries, min=-reach, max=reach).astype(held_as)


def setup_inputs(seed: int = 0) -> dict:
    streams_of = jax.random.split(jax.random.key(seed), 18)
    inputs = gaussian(streams_of[0], (TOKENS, D), 1.0, 6.0, ((0, 32),))
    image_count = draw_image_count(jax.random.fold_in(streams_of[17], 71), 0)
    rel_index = draw_rel_index(jax.random.fold_in(streams_of[17], 71), 0)
    rel_table = draw_rel_table(jax.random.fold_in(streams_of[17], 71), 0)
    norm1_gain = jnp.clip(1.0 + 0.1 * jax.random.normal(streams_of[4], (D,), jnp.float32), 0.5, 1.5)
    norm1_shift = gaussian(streams_of[5], (D,), 0.5, 3.0, (), jnp.float32)
    w_qkv = gaussian(streams_of[6], (3, D, D), D ** -0.5, 0.25, ((2, 4),))
    bias_qv = gaussian(streams_of[7], (2, D), 0.5, 3.0, ((1, 4),), jnp.float32)
    w_proj = gaussian(streams_of[8], (D, D), (D // 6) ** -0.5, 0.625, ((0, 4),))
    b_proj = gaussian(streams_of[9], (D,), 0.3, 2.0, (), jnp.float32)
    norm2_gain = jnp.clip(1.0 + 0.1 * jax.random.normal(streams_of[10], (D,), jnp.float32), 0.5, 1.5)
    norm2_shift = gaussian(streams_of[11], (D,), 0.5, 3.0, (), jnp.float32)
    w_fc1 = gaussian(streams_of[12], (D, FF), D ** -0.5, 0.25, ((1, 4),))
    b_fc1 = gaussian(streams_of[13], (FF,), 0.5, 3.0, ((0, 4),), jnp.float32)
    w_fc2 = gaussian(streams_of[14], (FF, D), (FF // 2) ** -0.5, 0.1875, ((0, 4),))
    b_fc2 = gaussian(streams_of[15], (D,), 0.3, 2.0, (), jnp.float32)
    out_grad = gaussian(streams_of[16], (TOKENS, D), 1.0, 6.0, ((0, 32),))
    return dict(inputs=inputs, image_count=image_count, rel_index=rel_index, rel_table=rel_table, norm1_gain=norm1_gain, norm1_shift=norm1_shift, w_qkv=w_qkv, bias_qv=bias_qv, w_proj=w_proj, b_proj=b_proj, norm2_gain=norm2_gain, norm2_shift=norm2_shift, w_fc1=w_fc1, b_fc1=b_fc1, w_fc2=w_fc2, b_fc2=b_fc2, out_grad=out_grad)


eps = 1e-05

def norm_forward(values, gain, shift):
    mean = lax.optimization_barrier(jnp.mean(values, axis=-1, keepdims=True))
    centred = values - mean
    var = lax.optimization_barrier(jnp.mean(centred * centred, axis=-1, keepdims=True))
    scale_inv = lax.rsqrt(var + eps)
    normed = centred * scale_inv
    return (normed * gain + shift, normed, scale_inv)

def norm_backward(grad, normed, scale_inv, gain):
    scaled = grad * gain
    return scale_inv * (scaled - lax.optimization_barrier(jnp.mean(scaled, axis=-1, keepdims=True)) - normed * lax.optimization_barrier(jnp.mean(scaled * normed, axis=-1, keepdims=True)))

def gelu_parts(pre):
    cdf = 0.5 * (1.0 + lax.erf(pre * 0.7071067811865476))
    dens = jnp.exp(-0.5 * pre * pre) * 0.3989422804014327
    return (pre * cdf, cdf + pre * dens)

def outer_dot(left, right):
    return lax.dot_general(left, right, (((0,), (0,)), ((), ())), preferred_element_type=jnp.float32)

def inner_t(left, right):
    return lax.dot_general(left, right, (((1,), (1,)), ((), ())), preferred_element_type=jnp.float32)

def reference(inputs, image_count, rel_index, rel_table, norm1_gain, norm1_shift, w_qkv, bias_qv, w_proj, b_proj, norm2_gain, norm2_shift, w_fc1, b_fc1, w_fc2, b_fc2, out_grad):
    group_rows = IMG_DEV * IMG_TOKENS
    nwin = group_rows // WINDOW
    scale = HEAD_DIM ** (-0.5)
    onehot = (rel_index[:, :, None] == jnp.arange(OFFSETS, dtype=jnp.int32)[None, None, :]).astype(jnp.float32)
    bias = jnp.einsum('qkt,th->hqk', onehot, rel_table, precision=lax.Precision.HIGHEST)
    xs = inputs.reshape(N_DP, group_rows, D)
    gs = out_grad.reshape(N_DP, group_rows, D)
    image_of_row = jnp.arange(group_rows, dtype=jnp.int32) // IMG_TOKENS

    def group_step(acc, packed):
        x_in, dy_in, count = packed
        live = (image_of_row < count).astype(jnp.float32)[:, None]
        x32 = x_in.astype(jnp.float32)
        xn1f, normed1, rs1 = norm_forward(x32, norm1_gain, norm1_shift)
        xn1 = xn1f.astype(jnp.bfloat16)
        qs = ((jnp.dot(xn1, w_qkv[0], preferred_element_type=jnp.float32) + bias_qv[0]) * scale).astype(jnp.bfloat16)
        kk = jnp.dot(xn1, w_qkv[1], preferred_element_type=jnp.float32).astype(jnp.bfloat16)
        vv = (jnp.dot(xn1, w_qkv[2], preferred_element_type=jnp.float32) + bias_qv[1]).astype(jnp.bfloat16)
        qw = qs.reshape(nwin, WINDOW, HEADS, HEAD_DIM).astype(jnp.float32)
        kw = kk.reshape(nwin, WINDOW, HEADS, HEAD_DIM).astype(jnp.float32)
        vw = vv.reshape(nwin, WINDOW, HEADS, HEAD_DIM).astype(jnp.float32)
        scores = jnp.einsum('nqhe,nkhe->nhqk', qw, kw) + bias[None]
        top = lax.optimization_barrier(jnp.max(scores, axis=-1, keepdims=True))
        lse = top + jnp.log(lax.optimization_barrier(jnp.sum(jnp.exp(scores - top), axis=-1, keepdims=True)))
        probs = jnp.exp(scores - lse)
        pb = probs.astype(jnp.bfloat16)
        att = jnp.einsum('nhqk,nkhe->nqhe', pb.astype(jnp.float32), vw)
        att_out = att.reshape(group_rows, D).astype(jnp.bfloat16)
        mid = x32 + (jnp.dot(att_out, w_proj, preferred_element_type=jnp.float32) + b_proj)
        xn2f, normed2, rs2 = norm_forward(mid, norm2_gain, norm2_shift)
        xn2 = xn2f.astype(jnp.bfloat16)
        pre = jnp.dot(xn2, w_fc1, preferred_element_type=jnp.float32) + b_fc1
        act, slope = gelu_parts(pre)
        hidden = act.astype(jnp.bfloat16)
        out = (live * (mid + jnp.dot(hidden, w_fc2, preferred_element_type=jnp.float32) + b_fc2)).astype(jnp.bfloat16)
        gout = dy_in.astype(jnp.float32) * live
        gout_b = gout.astype(jnp.bfloat16)
        g_b_fc2 = lax.optimization_barrier(jnp.sum(gout, axis=0))
        g_fc2 = outer_dot(hidden, gout_b)
        dpre = inner_t(gout_b, w_fc2) * slope
        g_b_fc1 = lax.optimization_barrier(jnp.sum(dpre, axis=0))
        dpre_b = dpre.astype(jnp.bfloat16)
        g_fc1 = outer_dot(xn2, dpre_b)
        dxn2 = inner_t(dpre_b, w_fc1)
        g_n2g = lax.optimization_barrier(jnp.sum(dxn2 * normed2, axis=0))
        g_n2s = lax.optimization_barrier(jnp.sum(dxn2, axis=0))
        dmid = gout + norm_backward(dxn2, normed2, rs2, norm2_gain)
        g_bp = lax.optimization_barrier(jnp.sum(dmid, axis=0))
        dmid_b = dmid.astype(jnp.bfloat16)
        g_proj = outer_dot(att_out, dmid_b)
        datt = inner_t(dmid_b, w_proj).astype(jnp.bfloat16)
        dw = datt.reshape(nwin, WINDOW, HEADS, HEAD_DIM).astype(jnp.float32)
        probs_again = jnp.exp(jnp.einsum('nqhe,nkhe->nhqk', qw, kw) + bias[None] - lse)
        pb2 = probs_again.astype(jnp.bfloat16).astype(jnp.float32)
        dvv = jnp.einsum('nhqk,nqhe->nkhe', pb2, dw)
        dprobs = jnp.einsum('nqhe,nkhe->nhqk', dw, vw)
        dscores = probs_again * (dprobs - lax.optimization_barrier(jnp.sum(probs_again * dprobs, axis=-1, keepdims=True)))
        g_tab = jnp.einsum('qkt,hqk->th', onehot, lax.optimization_barrier(jnp.sum(dscores, axis=0)), precision=lax.Precision.HIGHEST)
        dsb = dscores.astype(jnp.bfloat16).astype(jnp.float32)
        dq = (jnp.einsum('nhqk,nkhe->nqhe', dsb, kw) * scale).reshape(group_rows, D)
        dk = jnp.einsum('nhqk,nqhe->nkhe', dsb, qw).reshape(group_rows, D)
        dv = dvv.reshape(group_rows, D)
        g_bqv = jnp.stack([lax.optimization_barrier(jnp.sum(dq, axis=0)), lax.optimization_barrier(jnp.sum(dv, axis=0))])
        dqkv = jnp.stack([dq, dk, dv]).astype(jnp.bfloat16)
        g_qkv = jnp.stack([outer_dot(xn1, dqkv[c]) for c in range(3)])
        dxn1 = inner_t(dqkv[0], w_qkv[0]) + inner_t(dqkv[1], w_qkv[1]) + inner_t(dqkv[2], w_qkv[2])
        g_n1g = lax.optimization_barrier(jnp.sum(dxn1 * normed1, axis=0))
        g_n1s = lax.optimization_barrier(jnp.sum(dxn1, axis=0))
        dx = (dmid + norm_backward(dxn1, normed1, rs1, norm1_gain)).astype(jnp.bfloat16)
        terms = (g_tab, g_n1g, g_n1s, g_qkv, g_bqv, g_proj, g_bp, g_n2g, g_n2s, g_fc1, g_b_fc1, g_fc2, g_b_fc2)
        acc = tuple((a + t for a, t in zip(acc, terms)))
        return (acc, (out, dx))
    zero = (jnp.zeros((OFFSETS, HEADS), jnp.float32), jnp.zeros((D,), jnp.float32), jnp.zeros((D,), jnp.float32), jnp.zeros((3, D, D), jnp.float32), jnp.zeros((2, D), jnp.float32), jnp.zeros((D, D), jnp.float32), jnp.zeros((D,), jnp.float32), jnp.zeros((D,), jnp.float32), jnp.zeros((D,), jnp.float32), jnp.zeros((D, FF), jnp.float32), jnp.zeros((FF,), jnp.float32), jnp.zeros((FF, D), jnp.float32), jnp.zeros((D,), jnp.float32))
    acc, (outs, dxs) = lax.scan(group_step, zero, (xs, gs, image_count.astype(jnp.int32)))
    return (outs.reshape(TOKENS, D), dxs.reshape(TOKENS, D)) + acc
```

```python
import jax
import jax.numpy as jnp
from jax import lax
from jax.sharding import PartitionSpec as P

HEAD_DIM = 32
WINDOW = 49
OFFSETS = 169
IMG_TOKENS = 196


eps = 1e-05


def norm_forward(values, gain, shift):
    mean = jnp.mean(values, axis=-1, keepdims=True)
    centred = values - mean
    var = jnp.mean(centred * centred, axis=-1, keepdims=True)
    scale_inv = lax.rsqrt(var + eps)
    normed = centred * scale_inv
    return (normed * gain + shift, normed, scale_inv)


def norm_backward(grad, normed, scale_inv, gain):
    scaled = grad * gain
    return scale_inv * (
        scaled
        - jnp.mean(scaled, axis=-1, keepdims=True)
        - normed * jnp.mean(scaled * normed, axis=-1, keepdims=True)
    )


def gelu_parts(pre):
    cdf = 0.5 * (1.0 + lax.erf(pre * 0.7071067811865476))
    dens = jnp.exp(-0.5 * pre * pre) * 0.3989422804014327
    return (pre * cdf, cdf + pre * dens)


def outer_dot(left, right):
    return lax.dot_general(
        left, right, (((0,), (0,)), ((), ())), preferred_element_type=jnp.float32
    )


def inner_t(left, right):
    return lax.dot_general(
        left, right, (((1,), (1,)), ((), ())), preferred_element_type=jnp.float32
    )


def project_qkv(normed_rows, weights, biases, scale):
    qs = (
        (jnp.dot(normed_rows, weights[0], preferred_element_type=jnp.float32) + biases[0]) * scale
    ).astype(jnp.bfloat16)
    kk = jnp.dot(normed_rows, weights[1], preferred_element_type=jnp.float32).astype(jnp.bfloat16)
    vv = (jnp.dot(normed_rows, weights[2], preferred_element_type=jnp.float32) + biases[1]).astype(
        jnp.bfloat16
    )
    return (qs, kk, vv)


def window_attention(qs, kk, vv, bias, windows, heads):
    qw = qs.reshape(windows, WINDOW, heads, HEAD_DIM)
    kw = kk.reshape(windows, WINDOW, heads, HEAD_DIM)
    vw = vv.reshape(windows, WINDOW, heads, HEAD_DIM)
    scores = jnp.einsum("nqhe,nkhe->nhqk", qw, kw, preferred_element_type=jnp.float32) + bias[None]
    top = jnp.max(scores, axis=-1, keepdims=True)
    lse = top + jnp.log(jnp.sum(jnp.exp(scores - top), axis=-1, keepdims=True))
    pb = jnp.exp(scores - lse).astype(jnp.bfloat16)
    att = jnp.einsum("nhqk,nkhe->nqhe", pb, vw, preferred_element_type=jnp.float32)
    att_out = att.reshape(windows * WINDOW, heads * HEAD_DIM).astype(jnp.bfloat16)
    return (att_out, lse, qw, kw, vw)


def window_backward(datt, qw, kw, vw, bias, lse, onehot, scale):
    windows = qw.shape[0]
    heads = qw.shape[2]
    rows = windows * WINDOW
    width = heads * HEAD_DIM
    dw = datt.reshape(windows, WINDOW, heads, HEAD_DIM)
    probs_again = jnp.exp(
        jnp.einsum("nqhe,nkhe->nhqk", qw, kw, preferred_element_type=jnp.float32) + bias[None] - lse
    )
    pb_again = probs_again.astype(jnp.bfloat16)
    dvv = jnp.einsum("nhqk,nqhe->nkhe", pb_again, dw, preferred_element_type=jnp.float32)
    dprobs = jnp.einsum("nqhe,nkhe->nhqk", dw, vw, preferred_element_type=jnp.float32)
    dscores = probs_again * (dprobs - jnp.sum(probs_again * dprobs, axis=-1, keepdims=True))
    g_tab = jnp.einsum(
        "qkt,hqk->th", onehot, jnp.sum(dscores, axis=0), precision=lax.Precision.HIGHEST
    )
    dsb = dscores.astype(jnp.bfloat16)
    dq = (
        jnp.einsum("nhqk,nkhe->nqhe", dsb, kw, preferred_element_type=jnp.float32) * scale
    ).reshape(rows, width)
    dk = jnp.einsum("nhqk,nqhe->nkhe", dsb, qw, preferred_element_type=jnp.float32).reshape(
        rows, width
    )
    dv = dvv.reshape(rows, width)
    g_bqv = jnp.stack([jnp.sum(dq, axis=0), jnp.sum(dv, axis=0)])
    dqkv = jnp.stack([dq, dk, dv]).astype(jnp.bfloat16)
    return (g_tab, g_bqv, dqkv)


def gather_blocks(value):
    return lax.all_gather(value, "tensor", axis=0, tiled=False)


def local(
    inputs,
    image_count,
    rel_index,
    rel_table,
    norm1_gain,
    norm1_shift,
    w_qkv,
    bias_qv,
    w_proj,
    b_proj,
    norm2_gain,
    norm2_shift,
    w_fc1,
    b_fc1,
    w_fc2,
    b_fc2,
    out_grad,
):
    rows = inputs.shape[0]
    width = inputs.shape[1]
    shards = lax.axis_size("tensor")
    scale = HEAD_DIM ** (-0.5)
    row_ids = lax.axis_index("tensor") * rows + jnp.arange(rows, dtype=jnp.int32)
    live = (row_ids // IMG_TOKENS < image_count[0]).astype(jnp.float32)[:, None]
    onehot = (rel_index[:, :, None] == jnp.arange(OFFSETS, dtype=jnp.int32)[None, None, :]).astype(
        jnp.float32
    )
    wq_all = gather_blocks(w_qkv)
    wp_all = gather_blocks(w_proj)
    w1_all = gather_blocks(w_fc1)
    w2_all = gather_blocks(w_fc2)
    n_table = rel_table.size
    n_bqv = bias_qv.size
    small = gather_blocks(
        jnp.concatenate([rel_table.reshape(-1), bias_qv.reshape(-1), b_fc1.reshape(-1)])
    )
    table_all = small[:, :n_table].reshape(shards, *rel_table.shape)
    table_all = table_all.transpose(1, 0, 2).reshape(rel_table.shape[0], -1)
    bqv_all = small[:, n_table : n_table + n_bqv].reshape(shards, *bias_qv.shape)
    bqv_all = bqv_all.transpose(1, 0, 2).reshape(bias_qv.shape[0], -1)
    b1_all = small[:, n_table + n_bqv :].reshape(-1)
    wq_all = wq_all.transpose(1, 2, 0, 3).reshape(3, width, -1)
    wp_all = wp_all.reshape(-1, width)
    w1_all = w1_all.transpose(1, 0, 2).reshape(width, -1)
    w2_all = w2_all.reshape(-1, width)
    heads = table_all.shape[1]
    windows = rows // WINDOW

    x32 = inputs.astype(jnp.float32)
    xn1f, normed1, rs1 = norm_forward(x32, norm1_gain, norm1_shift)
    xn1 = xn1f.astype(jnp.bfloat16)
    gout = out_grad.astype(jnp.float32) * live
    gout_b = gout.astype(jnp.bfloat16)
    g_b_fc2 = jnp.sum(gout, axis=0)
    bias = jnp.einsum("qkt,th->hqk", onehot, table_all, precision=lax.Precision.HIGHEST)
    qs, kk, vv = project_qkv(xn1, wq_all, bqv_all, scale)
    att_out, lse, qw, kw, vw = window_attention(qs, kk, vv, bias, windows, heads)
    mid = x32 + (jnp.dot(att_out, wp_all, preferred_element_type=jnp.float32) + b_proj)
    xn2f, normed2, rs2 = norm_forward(mid, norm2_gain, norm2_shift)
    xn2 = xn2f.astype(jnp.bfloat16)
    pre = jnp.dot(xn2, w1_all, preferred_element_type=jnp.float32) + b1_all
    act, slope = gelu_parts(pre)
    hidden = act.astype(jnp.bfloat16)
    mlp = jnp.dot(hidden, w2_all, preferred_element_type=jnp.float32)
    outputs = (live * (mid + mlp + b_fc2)).astype(jnp.bfloat16)
    g_fc2 = outer_dot(hidden, gout_b)
    dpre = inner_t(gout_b, w2_all) * slope
    g_b_fc1 = jnp.sum(dpre, axis=0)
    dpre_b = dpre.astype(jnp.bfloat16)
    g_fc1 = outer_dot(xn2, dpre_b)
    dxn2 = inner_t(dpre_b, w1_all)
    g_n2g = jnp.sum(dxn2 * normed2, axis=0)
    g_n2s = jnp.sum(dxn2, axis=0)
    dmid = gout + norm_backward(dxn2, normed2, rs2, norm2_gain)
    g_bp = jnp.sum(dmid, axis=0)
    dmid_b = dmid.astype(jnp.bfloat16)
    g_proj = outer_dot(att_out, dmid_b)
    datt = inner_t(dmid_b, wp_all).astype(jnp.bfloat16)
    g_tab, g_bqv, dqkv = window_backward(datt, qw, kw, vw, bias, lse, onehot, scale)
    g_qkv = jnp.einsum("rd,cre->cde", xn1, dqkv, preferred_element_type=jnp.float32)
    dxn1 = jnp.einsum("cre,cde->rd", dqkv, wq_all, preferred_element_type=jnp.float32)
    g_n1g = jnp.sum(dxn1 * normed1, axis=0)
    g_n1s = jnp.sum(dxn1, axis=0)
    in_grad = (dmid + norm_backward(dxn1, normed1, rs1, norm1_gain)).astype(jnp.bfloat16)

    def blocks(value, axis):
        shape = value.shape[:axis] + (shards, value.shape[axis] // shards) + value.shape[axis + 1 :]
        return jnp.moveaxis(value.reshape(shape), axis, 0)

    def reduce_all(parts):
        flats = []
        for part in parts:
            flat = part.astype(jnp.bfloat16).reshape(shards, -1)
            flat = jnp.pad(flat, ((0, 0), (0, -flat.shape[1] % (16 * width))))
            flats.append(flat.reshape(shards, -1, width))
        sent = jnp.concatenate(flats, axis=1)
        own = lax.psum_scatter(
            sent.reshape(-1, width), "tensor", scatter_dimension=0, tiled=True
        )
        own = lax.psum(own, "dp").astype(jnp.float32)
        outs = []
        at = 0
        for part, flat in zip(parts, flats):
            size = part.size // shards
            piece = own[at : at + flat.shape[1]].reshape(-1)
            outs.append(piece[:size].reshape(part.shape[1:]))
            at += flat.shape[1]
        return outs

    g_fc1, g_fc2, g_b_fc1 = reduce_all([blocks(g_fc1, 1), blocks(g_fc2, 0), blocks(g_b_fc1, 0)])
    g_qkv, g_proj, g_tab, g_bqv = reduce_all(
        [blocks(g_qkv, 2), blocks(g_proj, 0), blocks(g_tab, 1), blocks(g_bqv, 1)]
    )
    g_n1g, g_n1s, g_bp, g_n2g, g_n2s, g_b_fc2 = lax.psum(
        (g_n1g, g_n1s, g_bp, g_n2g, g_n2s, g_b_fc2), ("dp", "tensor")
    )
    return (
        outputs,
        in_grad,
        g_tab,
        g_n1g,
        g_n1s,
        g_qkv,
        g_bqv,
        g_proj,
        g_bp,
        g_n2g,
        g_n2s,
        g_fc1,
        g_b_fc1,
        g_fc2,
        g_b_fc2,
    )


def solution(mesh):
    placed = (
        P(("dp", "tensor"), None),
        P("dp"),
        P(),
        P(None, "tensor"),
        P(),
        P(),
        P(None, None, "tensor"),
        P(None, "tensor"),
        P("tensor", None),
        P(),
        P(),
        P(),
        P(None, "tensor"),
        P("tensor"),
        P("tensor", None),
        P(),
        P(("dp", "tensor"), None),
    )
    return jax.shard_map(
        local,
        mesh=mesh,
        in_specs=placed,
        out_specs=(
            P(("dp", "tensor"), None),
            P(("dp", "tensor"), None),
            P(None, "tensor"),
            P(),
            P(),
            P(None, None, "tensor"),
            P(None, "tensor"),
            P("tensor", None),
            P(),
            P(),
            P(),
            P(None, "tensor"),
            P("tensor"),
            P("tensor", None),
            P(),
        ),
        check_vma=False,
    )
```

```python
import functools

import jax
import jax.numpy as jnp
from jax import lax
from jax.experimental import pallas as pl
from jax.experimental.pallas import tpu as pltpu
from jax.sharding import PartitionSpec as P


IMG_TOKENS = 196
ROW_TILE = 16
CHUNK = 256
FAR_BELOW = -1e30

eps = 1e-05
f32 = jnp.float32
bf16 = jnp.bfloat16


def norm_forward(values, gain, shift):
    mean = jnp.mean(values, axis=-1, keepdims=True)
    centred = values - mean
    var = jnp.mean(centred * centred, axis=-1, keepdims=True)
    scale_inv = lax.rsqrt(var + eps)
    normed = centred * scale_inv
    return (normed * gain + shift, normed, scale_inv)


def norm_backward(grad, normed, scale_inv, gain):
    scaled = grad * gain
    return scale_inv * (
        scaled
        - jnp.mean(scaled, axis=-1, keepdims=True)
        - normed * jnp.mean(scaled * normed, axis=-1, keepdims=True)
    )


def gelu_parts(pre):
    cdf = 0.5 * (1.0 + lax.erf(pre * 0.7071067811865476))
    dens = jnp.exp(-0.5 * pre * pre) * 0.3989422804014327
    return (pre * cdf, cdf + pre * dens)


def dot(left, right, left_dim, right_dim):
    return lax.dot_general(
        left, right, (((left_dim,), (right_dim,)), ((), ())), preferred_element_type=f32
    )


def head_masks(heads, width):
    head_of = lax.broadcasted_iota(jnp.int32, (1, width), 1) // (width // heads)
    return [(head_of == h).astype(f32) for h in range(heads)]


def spread(value, masks):
    return jnp.concatenate([value * mask.astype(bf16) for mask in masks], axis=0)


def fold(value, masks):
    rows = value.shape[0] // len(masks)
    total = value[:rows] * masks[0]
    for h in range(1, len(masks)):
        total = total + value[h * rows : (h + 1) * rows] * masks[h]
    return total


def each_window(windows, body):
    together = 4 if windows % 4 == 0 else 1

    def step(i, carry):
        for j in range(together):
            body(i * together + j)
        return carry

    lax.fori_loop(0, windows // together, step, 0)


def attend_kernel(heads, scale, xn_ref, w_ref, vec_ref, bias_ref, qkv_ref, p_ref, att_ref):
    _, windows, padded, width = qkv_ref.shape
    xn = xn_ref[...]

    def put(c, value):
        qkv_ref[c] = value.astype(bf16).reshape(windows, padded, width)

    put(0, (dot(xn, w_ref[0], 1, 0) + vec_ref[:, :width]) * scale)
    put(1, dot(xn, w_ref[1], 1, 0))
    put(2, dot(xn, w_ref[2], 1, 0) + vec_ref[:, width : 2 * width])
    masks = head_masks(heads, width)

    def window(w):
        scores = dot(qkv_ref[1, w], spread(qkv_ref[0, w], masks), 1, 1) + bias_ref[...]
        top = jnp.max(scores, axis=0, keepdims=True)
        powers = jnp.exp(scores - top)
        probs = powers * (1.0 / jnp.sum(powers, axis=0, keepdims=True))
        p_ref[w] = probs
        att = fold(dot(probs.astype(bf16), qkv_ref[2, w], 0, 0), masks)
        att_ref[w] = att.astype(bf16)

    each_window(windows, window)


def attend(xn, w, vec, bias, heads, scale, windows, padded):
    width = w.shape[2]
    lanes = heads * padded
    return pl.pallas_call(
        functools.partial(attend_kernel, heads, scale),
        out_shape=(
            jax.ShapeDtypeStruct((3, windows, padded, width), bf16),
            jax.ShapeDtypeStruct((windows, padded, lanes), f32),
            jax.ShapeDtypeStruct((windows, padded, width), bf16),
        ),
        name="attend",
        cost_estimate=pl.CostEstimate(
            flops=2 * xn.size * 3 * width, bytes_accessed=4 * xn.size, transcendentals=0
        ),
    )(xn, w, vec, bias)


def attend_back_kernel(
    heads,
    scale,
    dmid_ref,
    xn_ref,
    wp_ref,
    qkv_ref,
    p_ref,
    att_ref,
    dqkv_ref,
    g_ref,
    ds_ref,
    gb_ref,
    datt_ref,
):
    _, windows, padded, width = qkv_ref.shape
    dmid = dmid_ref[...]
    datt_ref[...] = dot(dmid, wp_ref[...], 1, 1).astype(bf16).reshape(windows, padded, width)
    ds_ref[...] = jnp.zeros_like(ds_ref)
    gb_ref[...] = jnp.zeros_like(gb_ref)
    masks = head_masks(heads, width)

    def window(w):
        probs = p_ref[w]
        spread_d = spread(datt_ref[w], masks)
        dv = dot(probs.astype(bf16), spread_d, 1, 0)
        dprobs = dot(qkv_ref[2, w], spread_d, 1, 1)
        dscores = probs * (dprobs - jnp.sum(probs * dprobs, axis=0, keepdims=True))
        ds_ref[...] += dscores
        ds_b = dscores.astype(bf16)
        dk = dot(ds_b, spread(qkv_ref[0, w], masks), 1, 0)
        dq = fold(dot(ds_b, qkv_ref[1, w], 0, 0), masks) * scale
        dqkv_ref[w] = jnp.concatenate([dq, dk, dv], axis=1).astype(bf16)
        gb_ref[0:1, :] += jnp.sum(dq, axis=0, keepdims=True)
        gb_ref[1:2, :] += jnp.sum(dv, axis=0, keepdims=True)

    each_window(windows, window)
    dqkv = dqkv_ref[...].reshape(windows * padded, 3 * width)
    g_ref[:, : 3 * width] = dot(xn_ref[...], dqkv, 0, 0).astype(bf16)
    g_ref[:, 3 * width :] = dot(dmid, att_ref[...], 0, 0).astype(bf16)


def attend_back(dmid, xn, wp, qkv, probs, att, heads, scale):
    _, windows, padded, width = qkv.shape
    return pl.pallas_call(
        functools.partial(attend_back_kernel, heads, scale),
        out_shape=(
            jax.ShapeDtypeStruct((windows, padded, 3 * width), bf16),
            jax.ShapeDtypeStruct((dmid.shape[1], 4 * width), bf16),
            jax.ShapeDtypeStruct(probs.shape[1:], f32),
            jax.ShapeDtypeStruct((2, width), f32),
        ),
        scratch_shapes=[pltpu.VMEM((windows, padded, width), bf16)],
        name="attend_back",
        cost_estimate=pl.CostEstimate(
            flops=2 * dmid.size * 8 * width, bytes_accessed=4 * dmid.size, transcendentals=0
        ),
    )(dmid, xn, wp, qkv, probs, att)


def mlp_kernel(
    offset, xn_ref, gout_ref, w1_ref, vec_ref, w2_ref, hidden_ref, dpre_ref, gb_ref, g_ref, sum_ref
):
    ff = w1_ref.shape[1]

    @pl.when(pl.program_id(0) == 0)
    def _():
        gb_ref[...] = jnp.zeros_like(gb_ref)
        sum_ref[...] = jnp.zeros_like(sum_ref)

    xn = xn_ref[...]
    gout = gout_ref[...]
    pre = dot(xn, w1_ref[...], 1, 0) + vec_ref[:, offset:]
    act, slope = gelu_parts(pre)
    hidden = act.astype(bf16)
    hidden_ref[...] = hidden
    dpre = dot(gout, w2_ref[...], 1, 1) * slope
    gb_ref[...] += jnp.sum(dpre, axis=0, keepdims=True)
    dpre_b = dpre.astype(bf16)
    dpre_ref[...] = dpre_b
    sum_ref[:ff] += dot(dpre_b, xn, 0, 0)
    sum_ref[ff:] += dot(hidden, gout, 0, 0)

    @pl.when(pl.program_id(0) == pl.num_programs(0) - 1)
    def _():
        g_ref[...] = sum_ref[...].astype(bf16)


def split_kernel(parts, digit_ref, *refs):
    pieces = refs[parts:]
    rows = pieces[0].shape[0]
    for j, piece in enumerate(pieces):
        start = pl.multiple_of((digit_ref[0] ^ j) * rows, rows)
        total = refs[0][pl.ds(start, rows), :].astype(f32)
        for ref in refs[1:parts]:
            total = total + ref[pl.ds(start, rows), :].astype(f32)
        piece[...] = total.astype(bf16)


def split(values, digit, ways):
    rows, width = values[0].shape
    return pl.pallas_call(
        functools.partial(split_kernel, len(values)),
        in_specs=[pl.BlockSpec(memory_space=pltpu.SMEM)]
        + [pl.BlockSpec(memory_space=pltpu.VMEM)] * len(values),
        out_shape=[shape_of((rows // ways, width), bf16)] * ways,
        name="split",
    )(digit, *values)


def merge_kernel(ways, digit_ref, *refs):
    out_ref = refs[ways]
    rows = refs[0].shape[0]
    for j in range(ways):
        start = pl.multiple_of((digit_ref[0] ^ j) * rows, rows)
        out_ref[pl.ds(start, rows), :] = refs[j][...].astype(out_ref.dtype)


def merge(pieces, digit, dtype):
    ways = len(pieces)
    rows, width = pieces[0].shape
    return pl.pallas_call(
        functools.partial(merge_kernel, ways),
        in_specs=[pl.BlockSpec(memory_space=pltpu.SMEM)]
        + [pl.BlockSpec(memory_space=pltpu.VMEM)] * ways,
        out_shape=shape_of((rows * ways, width), dtype),
        name="merge",
    )(digit, *pieces)


def by_rows(kernel, rows, cut, whole, cut_outs, whole_outs, flops, scratch=()):
    chunk = CHUNK if rows % CHUNK == 0 else rows

    def cut_spec(value):
        return pl.BlockSpec((chunk,) + value.shape[1:], lambda i: (i,) + (0,) * (value.ndim - 1))

    def whole_spec(value):
        return pl.BlockSpec(value.shape, lambda i: (0,) * value.ndim)

    return pl.pallas_call(
        kernel,
        grid=(rows // chunk,),
        in_specs=[cut_spec(v) for v in cut] + [whole_spec(v) for v in whole],
        out_specs=[cut_spec(v) for v in cut_outs] + [whole_spec(v) for v in whole_outs],
        out_shape=list(cut_outs) + list(whole_outs),
        scratch_shapes=list(scratch),
        cost_estimate=pl.CostEstimate(
            flops=flops,
            bytes_accessed=sum(v.size * v.dtype.itemsize for v in cut),
            transcendentals=0,
        ),
    )(*cut, *whole)


def shape_of(shape, dtype=f32):
    return jax.ShapeDtypeStruct(shape, dtype)


def enter_kernel(count, *refs):
    x_ref, atts = refs[0], refs[1 : 1 + count]
    b_ref, gain_ref, shift_ref = refs[1 + count : 4 + count]
    weights = refs[4 + count : 4 + 2 * count]
    mid_ref, xn_ref = refs[4 + 2 * count :]
    total = dot(atts[0][...], weights[0][...], 1, 0)
    for att, weight in zip(atts[1:], weights[1:]):
        total = total + dot(att[...], weight[...], 1, 0)
    mid = x_ref[...].astype(f32) + (total + b_ref[...])
    mid_ref[...] = mid
    xn_ref[...] = norm_forward(mid, gain_ref[...], shift_ref[...])[0].astype(bf16)


def leave_kernel(count, *refs):
    mid_ref, hiddens = refs[0], refs[1 : 1 + count]
    b_ref, weights = refs[1 + count], refs[2 + count : 2 + 2 * count]
    out_ref = refs[2 + 2 * count]
    total = dot(hiddens[0][...], weights[0][...], 1, 0)
    for hidden, weight in zip(hiddens[1:], weights[1:]):
        total = total + dot(hidden[...], weight[...], 1, 0)
    out_ref[...] = (mid_ref[...] + total + b_ref[...]).astype(bf16)


def mid_back_kernel(count, *refs):
    mid_ref, gout_ref = refs[:2]
    dpres = refs[2 : 2 + count]
    gain_ref, shift_ref = refs[2 + count : 4 + count]
    weights = refs[4 + count : 4 + 2 * count]
    dmid_ref, dmid_b_ref, sums_ref = refs[4 + 2 * count :]

    @pl.when(pl.program_id(0) == 0)
    def _():
        sums_ref[...] = jnp.zeros_like(sums_ref)

    dxn = dot(dpres[0][...], weights[0][...], 1, 1)
    for dpre, weight in zip(dpres[1:], weights[1:]):
        dxn = dxn + dot(dpre[...], weight[...], 1, 1)
    gain = gain_ref[...]
    _, normed, scale_inv = norm_forward(mid_ref[...], gain, shift_ref[...])
    gout = gout_ref[...].astype(f32)
    dmid = gout + norm_backward(dxn, normed, scale_inv, gain)
    dmid_ref[...] = dmid
    dmid_b_ref[...] = dmid.astype(bf16)
    for at, value in enumerate((dxn * normed, dxn, dmid, gout)):
        sums_ref[at : at + 1, :] += jnp.sum(value, axis=0, keepdims=True)


def in_back_kernel(count, *refs):
    x_ref, dmid_ref = refs[:2]
    grads = refs[2 : 2 + count]
    gain_ref, shift_ref = refs[2 + count : 4 + count]
    weights = refs[4 + count : 4 + 2 * count]
    out_ref, sums_ref = refs[4 + 2 * count :]

    @pl.when(pl.program_id(0) == 0)
    def _():
        sums_ref[...] = jnp.zeros_like(sums_ref)

    dxn = jnp.zeros(dmid_ref.shape, f32)
    for at in range(count):
        for c in range(3):
            cols = weights[at].shape[2]
            dxn = dxn + dot(grads[at][:, c * cols : (c + 1) * cols], weights[at][c], 1, 1)
    gain = gain_ref[...]
    _, normed, scale_inv = norm_forward(x_ref[...].astype(f32), gain, shift_ref[...])
    out_ref[...] = (dmid_ref[...] + norm_backward(dxn, normed, scale_inv, gain)).astype(bf16)
    for at, value in enumerate((dxn * normed, dxn)):
        sums_ref[at : at + 1, :] += jnp.sum(value, axis=0, keepdims=True)


def local(
    inputs,
    image_count,
    rel_index,
    rel_table,
    norm1_gain,
    norm1_shift,
    w_qkv,
    bias_qv,
    w_proj,
    b_proj,
    norm2_gain,
    norm2_shift,
    w_fc1,
    b_fc1,
    w_fc2,
    b_fc2,
    out_grad,
):
    rows, width = inputs.shape
    window = rel_index.shape[0]
    offsets, heads = rel_table.shape
    shards = lax.axis_size("tensor")
    me = lax.axis_index("tensor")
    head_dim = w_qkv.shape[2] // heads
    scale = head_dim ** (-0.5)
    windows = rows // window
    padded = -(-window // ROW_TILE) * ROW_TILE
    n = windows * padded
    row = lambda value: value.reshape(1, -1)

    def swap(value, bit):
        return lax.ppermute(value, "tensor", [(i, i ^ bit) for i in range(shards)])

    def gather(value):
        got = [value]
        for m in range(1, shards):
            low = m & -m
            got.append(swap(got[m ^ low], low))
        return got

    def pad_rows(value):
        value = value.reshape(windows, window, -1)
        return jnp.pad(value, ((0, 0), (0, padded - window), (0, 0))).reshape(n, -1)

    def cut_rows(value):
        return value.reshape(windows, padded, -1)[:, :window].reshape(rows, -1)

    index = jnp.pad(
        rel_index, ((0, padded - window), (0, padded - window)), constant_values=-1
    )
    onehot = (index[:, :, None] == jnp.arange(offsets, dtype=jnp.int32)).astype(f32)
    bias = jnp.einsum("qkt,th->khq", onehot, rel_table, precision=lax.Precision.HIGHEST)
    keys = jnp.arange(padded, dtype=jnp.int32)[:, None, None]
    bias = jnp.where(keys < window, bias, FAR_BELOW).reshape(padded, heads * padded)

    biases = gather(bias)
    vectors = gather(row(jnp.concatenate([bias_qv.reshape(-1), b_fc1])))
    wqs = gather(w_qkv)
    wps = gather(w_proj)
    w1s = gather(w_fc1)
    w2s = gather(w_fc2)

    row_ids = me * rows + jnp.arange(rows, dtype=jnp.int32)
    live = (row_ids // IMG_TOKENS < image_count[0])[:, None]
    xn1 = norm_forward(inputs.astype(f32), norm1_gain, norm1_shift)[0].astype(bf16)
    xn1 = pad_rows(xn1)
    x_pad = pad_rows(inputs)
    gout = pad_rows(jnp.where(live, out_grad, jnp.zeros_like(out_grad)))

    order = range(shards)
    qkvs, probs, atts = [], [], []
    for m in order:
        qkv, p, att = attend(xn1, wqs[m], vectors[m], biases[m], heads, scale, windows, padded)
        qkvs.append(qkv)
        probs.append(p)
        atts.append(att.reshape(n, -1))

    mid, xn2 = by_rows(
        functools.partial(enter_kernel, shards),
        n,
        [x_pad] + atts,
        [row(b_proj), row(norm2_gain), row(norm2_shift)] + wps,
        [shape_of((n, width)), shape_of((n, width), bf16)],
        [],
        2 * n * width * width,
    )

    ff = w_fc1.shape[1]
    hiddens, dpres, g_b1s, g_fcs = {}, {}, {}, {}
    back_order = list(reversed(order))
    for m in back_order:
        hiddens[m], dpres[m], g_b1s[m], g_fcs[m] = by_rows(
            functools.partial(mlp_kernel, bias_qv.size),
            n,
            [xn2, gout],
            [w1s[m], vectors[m], w2s[m]],
            [shape_of((n, ff), bf16), shape_of((n, ff), bf16)],
            [shape_of((1, ff)), shape_of((2 * ff, width), bf16)],
            8 * n * width * ff,
            [pltpu.VMEM((2 * ff, width), f32)],
        )

    def scatter(parts):
        held = {m: [parts[m]] for m in parts}
        for m in range(shards - 1, 0, -1):
            low = m & -m
            total = held[m][0]
            for term in held[m][1:]:
                total = total + term
            held[m ^ low].append(swap(total, low))
        return held[0]

    groups = lax.axis_size("dp")
    group = lax.axis_index("dp")

    def swap_dp(value, bits):
        return lax.ppermute(value, "dp", [(i, i ^ bits) for i in range(groups)])

    def swap_all(pieces, stride):
        got = []
        for j, piece in enumerate(pieces):
            got.append(swap_dp(piece, j * stride) if j else piece)
        return got

    def sum_dp(terms, ways):
        stages = []
        stride = 1
        for way in ways:
            stages.append((stride, way, (group // stride % way).reshape(1)))
            stride *= way
        for stride, way, digit in stages:
            terms = swap_all(split(terms, digit, way), stride)
        total = terms[0].astype(f32)
        for term in terms[1:]:
            total = total + term.astype(f32)
        total = total.astype(bf16)
        for at, (stride, way, digit) in reversed(list(enumerate(stages))):
            pieces = swap_all([total] * way, stride)
            total = merge(pieces, digit, f32 if at == 0 else bf16)
        return total

    def ways_of(most):
        left = groups
        ways = []
        while left > 1:
            ways.append(min(most[min(len(ways), len(most) - 1)], left))
            left //= ways[-1]
        return ways

    g_fc = sum_dp(scatter(g_fcs), ways_of((2, 4)))
    g_fc1, g_fc2 = g_fc[:ff].T, g_fc[ff:]

    listed = lambda parts: [parts[m] for m in order]
    dmid, dmid_b, sums2 = by_rows(
        functools.partial(mid_back_kernel, shards),
        n,
        [mid, gout] + listed(dpres),
        [row(norm2_gain), row(norm2_shift)] + w1s,
        [shape_of((n, width)), shape_of((n, width), bf16)],
        [shape_of((8, width))],
        2 * n * width * ff * shards,
    )

    dqkvs, dss, g_bqvs, g_atts = {}, {}, {}, {}
    for m in back_order:
        dqkv, g_atts[m], dss[m], g_bqvs[m] = attend_back(
            dmid_b, xn1, wps[m], qkvs[m], probs[m], atts[m], heads, scale
        )
        dqkvs[m] = dqkv.reshape(n, -1)
    g_att = sum_dp(scatter(g_atts), ways_of((8,)))
    cols = w_qkv.shape[2]
    g_qkv = jnp.stack([g_att[:, c * cols : (c + 1) * cols] for c in range(3)])
    g_proj = g_att[:, 3 * cols :].T

    in_grad, sums1 = by_rows(
        functools.partial(in_back_kernel, shards),
        n,
        [x_pad, dmid] + listed(dqkvs),
        [row(norm1_gain), row(norm1_shift)] + wqs,
        [shape_of((n, width), bf16)],
        [shape_of((8, width))],
        6 * n * width * width,
    )
    (outputs,) = by_rows(
        functools.partial(leave_kernel, shards),
        n,
        [mid] + listed(hiddens),
        [row(b_fc2)] + w2s,
        [shape_of((n, width), bf16)],
        [],
        2 * n * width * ff * shards,
    )
    outputs = cut_rows(outputs)
    outputs = jnp.where(live, outputs, jnp.zeros_like(outputs))
    in_grad = cut_rows(in_grad)

    ds_all = jnp.stack(listed(dss)).reshape(shards, padded, heads, padded)
    g_tabs = jnp.einsum(
        "qkt,mkhq->mth", onehot, ds_all, precision=lax.Precision.HIGHEST
    )
    per_shard = jnp.concatenate(
        [
            g_tabs.reshape(shards, -1),
            jnp.stack(listed(g_bqvs)).reshape(shards, -1),
            jnp.stack(listed(g_b1s)).reshape(shards, -1),
        ],
        axis=1,
    )
    shared = jnp.concatenate([sums2[:4].reshape(-1), sums1[:2].reshape(-1)])
    per_shard = jnp.concatenate(
        [per_shard, jnp.broadcast_to(shared, (shards, shared.size))], axis=1
    )
    small = sum(scatter({m: per_shard[m] for m in order}))
    bit = 1
    while bit < groups:
        small = small + swap_dp(small, bit)
        bit *= 2
    pieces = []
    at = 0
    for shape in (rel_table.shape, bias_qv.shape, b_fc1.shape) + ((width,),) * 6:
        size = 1
        for extent in shape:
            size *= extent
        pieces.append(small[at : at + size].reshape(shape))
        at += size
    g_tab, g_bqv, g_b_fc1, g_n2g, g_n2s, g_bp, g_b_fc2, g_n1g, g_n1s = pieces
    return (
        outputs,
        in_grad,
        g_tab,
        g_n1g,
        g_n1s,
        g_qkv,
        g_bqv,
        g_proj,
        g_bp,
        g_n2g,
        g_n2s,
        g_fc1,
        g_b_fc1,
        g_fc2,
        g_b_fc2,
    )


def solution(mesh):
    placed = (
        P(("dp", "tensor"), None),
        P("dp"),
        P(),
        P(None, "tensor"),
        P(),
        P(),
        P(None, None, "tensor"),
        P(None, "tensor"),
        P("tensor", None),
        P(),
        P(),
        P(),
        P(None, "tensor"),
        P("tensor"),
        P("tensor", None),
        P(),
        P(("dp", "tensor"), None),
    )
    return jax.shard_map(
        local,
        mesh=mesh,
        in_specs=placed,
        out_specs=(
            P(("dp", "tensor"), None),
            P(("dp", "tensor"), None),
            P(None, "tensor"),
            P(),
            P(),
            P(None, None, "tensor"),
            P(None, "tensor"),
            P("tensor", None),
            P(),
            P(),
            P(),
            P(None, "tensor"),
            P("tensor"),
            P("tensor", None),
            P(),
        ),
        check_vma=False,
    )
```

```python
import functools

import jax
import jax.numpy as jnp
from jax import lax
from jax.experimental import pallas as pl
from jax.experimental.pallas import tpu as pltpu
from jax.sharding import PartitionSpec as P


IMG_TOKENS = 196
ROW_TILE = 16
CHUNK = 256
TOGETHER = 4
FAR_BELOW = -1e30

eps = 1e-05
f32 = jnp.float32
bf16 = jnp.bfloat16


def norm_forward(values, gain, shift):
    mean = jnp.mean(values, axis=-1, keepdims=True)
    centred = values - mean
    var = jnp.mean(centred * centred, axis=-1, keepdims=True)
    scale_inv = lax.rsqrt(var + eps)
    normed = centred * scale_inv
    return (normed * gain + shift, normed, scale_inv)


def norm_backward(grad, normed, scale_inv, gain):
    scaled = grad * gain
    return scale_inv * (
        scaled
        - jnp.mean(scaled, axis=-1, keepdims=True)
        - normed * jnp.mean(scaled * normed, axis=-1, keepdims=True)
    )


def gelu_parts(pre):
    cdf = 0.5 * (1.0 + lax.erf(pre * 0.7071067811865476))
    dens = jnp.exp(-0.5 * pre * pre) * 0.3989422804014327
    return (pre * cdf, cdf + pre * dens)


def dot(left, right, left_dim, right_dim):
    return lax.dot_general(
        left, right, (((left_dim,), (right_dim,)), ((), ())), preferred_element_type=f32
    )


def head_masks(heads, width):
    head_of = lax.broadcasted_iota(jnp.int32, (1, width), 1) // (width // heads)
    return [(head_of == h).astype(f32) for h in range(heads)]


def spread(value, masks):
    return jnp.concatenate([value * mask.astype(bf16) for mask in masks], axis=0)


def fold(value, masks):
    rows = value.shape[0] // len(masks)
    total = value[:rows] * masks[0]
    for h in range(1, len(masks)):
        total = total + value[h * rows : (h + 1) * rows] * masks[h]
    return total


def each_window(windows, body):
    together = TOGETHER if windows % TOGETHER == 0 else 1

    def step(i, carry):
        body([i * together + j for j in range(together)])
        return carry

    lax.fori_loop(0, windows // together, step, 0)


def attend_kernel(heads, scale, xn_ref, w_ref, vec_ref, bias_ref, qkv_ref, p_ref, att_ref):
    _, windows, padded, width = qkv_ref.shape
    xn = xn_ref[...]

    def put(c, value):
        qkv_ref[c] = value.astype(bf16).reshape(windows, padded, width)

    put(0, (dot(xn, w_ref[0], 1, 0) + vec_ref[:, :width]) * scale)
    put(1, dot(xn, w_ref[1], 1, 0))
    put(2, dot(xn, w_ref[2], 1, 0) + vec_ref[:, width : 2 * width])
    masks = head_masks(heads, width)

    def some(ws):
        queries = [spread(qkv_ref[0, w], masks) for w in ws]
        scores = [dot(qkv_ref[1, w], q, 1, 1) + bias_ref[...] for w, q in zip(ws, queries)]
        tops = [jnp.max(x, axis=0, keepdims=True) for x in scores]
        powers = [jnp.exp(x - top) for x, top in zip(scores, tops)]
        sums = [jnp.sum(x, axis=0, keepdims=True) for x in powers]
        probs = [x * (1.0 / total) for x, total in zip(powers, sums)]
        outs = [dot(x.astype(bf16), qkv_ref[2, w], 0, 0) for w, x in zip(ws, probs)]
        for w, x, out in zip(ws, probs, outs):
            p_ref[w] = x
            att_ref[w] = fold(out, masks).astype(bf16)

    each_window(windows, some)


def attend(xn, w, vec, bias, heads, scale, windows, padded):
    width = w.shape[2]
    lanes = heads * padded
    return pl.pallas_call(
        functools.partial(attend_kernel, heads, scale),
        out_shape=(
            jax.ShapeDtypeStruct((3, windows, padded, width), bf16),
            jax.ShapeDtypeStruct((windows, padded, lanes), f32),
            jax.ShapeDtypeStruct((windows, padded, width), bf16),
        ),
        name="attend",
        cost_estimate=pl.CostEstimate(
            flops=2 * xn.size * 3 * width, bytes_accessed=4 * xn.size, transcendentals=0
        ),
    )(xn, w, vec, bias)


def attend_back_kernel(
    heads,
    scale,
    dmid_ref,
    xn_ref,
    wp_ref,
    qkv_ref,
    p_ref,
    att_ref,
    dqkv_ref,
    g_ref,
    ds_ref,
    gb_ref,
    datt_ref,
):
    _, windows, padded, width = qkv_ref.shape
    dmid = dmid_ref[...]
    datt_ref[...] = dot(dmid, wp_ref[...], 1, 1).astype(bf16).reshape(windows, padded, width)
    ds_ref[...] = jnp.zeros_like(ds_ref)
    gb_ref[...] = jnp.zeros_like(gb_ref)
    masks = head_masks(heads, width)

    def some(ws):
        probs = [p_ref[w] for w in ws]
        grads = [spread(datt_ref[w], masks) for w in ws]
        dprobs = [dot(qkv_ref[2, w], d, 1, 1) for w, d in zip(ws, grads)]
        dvs = [dot(x.astype(bf16), d, 1, 0) for x, d in zip(probs, grads)]
        inner = [jnp.sum(x * dx, axis=0, keepdims=True) for x, dx in zip(probs, dprobs)]
        dscores = [x * (dx - total) for x, dx, total in zip(probs, dprobs, inner)]
        ds_b = [x.astype(bf16) for x in dscores]
        queries = [spread(qkv_ref[0, w], masks) for w in ws]
        dks = [dot(x, q, 1, 0) for x, q in zip(ds_b, queries)]
        dqs = [fold(dot(x, qkv_ref[1, w], 0, 0), masks) * scale for w, x in zip(ws, ds_b)]
        for w, dq, dk, dv in zip(ws, dqs, dks, dvs):
            dqkv_ref[w] = jnp.concatenate([dq, dk, dv], axis=1).astype(bf16)
        ds_ref[...] += sum(dscores)
        gb_ref[0:1, :] += jnp.sum(sum(dqs), axis=0, keepdims=True)
        gb_ref[1:2, :] += jnp.sum(sum(dvs), axis=0, keepdims=True)

    each_window(windows, some)
    dqkv = dqkv_ref[...].reshape(windows * padded, 3 * width)
    g_ref[:, : 3 * width] = dot(xn_ref[...], dqkv, 0, 0).astype(bf16)
    g_ref[:, 3 * width :] = dot(dmid, att_ref[...], 0, 0).astype(bf16)


def attend_back(dmid, xn, wp, qkv, probs, att, heads, scale):
    _, windows, padded, width = qkv.shape
    return pl.pallas_call(
        functools.partial(attend_back_kernel, heads, scale),
        out_shape=(
            jax.ShapeDtypeStruct((windows, padded, 3 * width), bf16),
            jax.ShapeDtypeStruct((dmid.shape[1], 4 * width), bf16),
            jax.ShapeDtypeStruct(probs.shape[1:], f32),
            jax.ShapeDtypeStruct((2, width), f32),
        ),
        scratch_shapes=[pltpu.VMEM((windows, padded, width), bf16)],
        name="attend_back",
        cost_estimate=pl.CostEstimate(
            flops=2 * dmid.size * 8 * width, bytes_accessed=4 * dmid.size, transcendentals=0
        ),
    )(dmid, xn, wp, qkv, probs, att)


def mlp_kernel(
    offset, xn_ref, gout_ref, w1_ref, vec_ref, w2_ref, hidden_ref, dpre_ref, gb_ref, g_ref, sum_ref
):
    ff = w1_ref.shape[1]

    @pl.when(pl.program_id(0) == 0)
    def _():
        gb_ref[...] = jnp.zeros_like(gb_ref)
        sum_ref[...] = jnp.zeros_like(sum_ref)

    xn = xn_ref[...]
    gout = gout_ref[...]
    pre = dot(xn, w1_ref[...], 1, 0) + vec_ref[:, offset:]
    act, slope = gelu_parts(pre)
    hidden = act.astype(bf16)
    hidden_ref[...] = hidden
    dpre = dot(gout, w2_ref[...], 1, 1) * slope
    gb_ref[...] += jnp.sum(dpre, axis=0, keepdims=True)
    dpre_b = dpre.astype(bf16)
    dpre_ref[...] = dpre_b
    sum_ref[:ff] += dot(dpre_b, xn, 0, 0)
    sum_ref[ff:] += dot(hidden, gout, 0, 0)

    @pl.when(pl.program_id(0) == pl.num_programs(0) - 1)
    def _():
        g_ref[...] = sum_ref[...].astype(bf16)


def split_kernel(parts, digit_ref, *refs):
    pieces = refs[parts:]
    rows = pieces[0].shape[0]
    for j, piece in enumerate(pieces):
        start = pl.multiple_of((digit_ref[0] ^ j) * rows, rows)
        total = refs[0][pl.ds(start, rows), :].astype(f32)
        for ref in refs[1:parts]:
            total = total + ref[pl.ds(start, rows), :].astype(f32)
        piece[...] = total.astype(bf16)


def split(values, digit, ways):
    rows, width = values[0].shape
    return pl.pallas_call(
        functools.partial(split_kernel, len(values)),
        in_specs=[pl.BlockSpec(memory_space=pltpu.SMEM)]
        + [pl.BlockSpec(memory_space=pltpu.VMEM)] * len(values),
        out_shape=[shape_of((rows // ways, width), bf16)] * ways,
        name="split",
    )(digit, *values)


def merge_kernel(ways, digit_ref, *refs):
    out_ref = refs[-1]
    rows = refs[0].shape[0]
    for j in range(ways):
        start = pl.multiple_of((digit_ref[0] ^ j) * rows, rows)
        out_ref[pl.ds(start, rows), :] = refs[j][...].astype(out_ref.dtype)
    if len(refs) == ways + 1:
        return
    first, second = refs[ways : ways + 2]
    if len(first.shape) == 3:
        cols = first.shape[2]
        for c in range(3):
            first[c] = out_ref[:, c * cols : (c + 1) * cols]
        second[...] = out_ref[:, 3 * cols :].T
    else:
        ff = second.shape[0]
        first[...] = out_ref[:ff, :].T
        second[...] = out_ref[ff:, :]


def merge(pieces, digit, results):
    ways = len(pieces)
    rows, width = pieces[0].shape
    whole = (rows * ways, width)
    return pl.pallas_call(
        functools.partial(merge_kernel, ways),
        in_specs=[pl.BlockSpec(memory_space=pltpu.SMEM)]
        + [pl.BlockSpec(memory_space=pltpu.VMEM)] * ways,
        out_shape=[shape_of(r) for r in results] if results else shape_of(whole, bf16),
        scratch_shapes=[pltpu.VMEM(whole, f32)] if results else [],
        name="merge",
    )(digit, *pieces)


def by_rows(kernel, rows, cut, whole, cut_outs, whole_outs, flops, scratch=()):
    chunk = CHUNK if rows % CHUNK == 0 else rows

    def cut_spec(value):
        return pl.BlockSpec((chunk,) + value.shape[1:], lambda i: (i,) + (0,) * (value.ndim - 1))

    def whole_spec(value):
        return pl.BlockSpec(value.shape, lambda i: (0,) * value.ndim)

    return pl.pallas_call(
        kernel,
        grid=(rows // chunk,),
        in_specs=[cut_spec(v) for v in cut] + [whole_spec(v) for v in whole],
        out_specs=[cut_spec(v) for v in cut_outs] + [whole_spec(v) for v in whole_outs],
        out_shape=list(cut_outs) + list(whole_outs),
        scratch_shapes=list(scratch),
        cost_estimate=pl.CostEstimate(
            flops=flops,
            bytes_accessed=sum(v.size * v.dtype.itemsize for v in cut),
            transcendentals=0,
        ),
    )(*cut, *whole)


def shape_of(shape, dtype=f32):
    return jax.ShapeDtypeStruct(shape, dtype)


def enter_kernel(count, *refs):
    x_ref, atts = refs[0], refs[1 : 1 + count]
    b_ref, gain_ref, shift_ref = refs[1 + count : 4 + count]
    weights = refs[4 + count : 4 + 2 * count]
    mid_ref, xn_ref = refs[4 + 2 * count :]
    total = dot(atts[0][...], weights[0][...], 1, 0)
    for att, weight in zip(atts[1:], weights[1:]):
        total = total + dot(att[...], weight[...], 1, 0)
    mid = x_ref[...].astype(f32) + (total + b_ref[...])
    mid_ref[...] = mid
    xn_ref[...] = norm_forward(mid, gain_ref[...], shift_ref[...])[0].astype(bf16)


def leave_kernel(count, *refs):
    mid_ref, hiddens = refs[0], refs[1 : 1 + count]
    b_ref, weights = refs[1 + count], refs[2 + count : 2 + 2 * count]
    out_ref = refs[2 + 2 * count]
    total = dot(hiddens[0][...], weights[0][...], 1, 0)
    for hidden, weight in zip(hiddens[1:], weights[1:]):
        total = total + dot(hidden[...], weight[...], 1, 0)
    out_ref[...] = (mid_ref[...] + total + b_ref[...]).astype(bf16)


def mid_back_kernel(count, *refs):
    mid_ref, gout_ref = refs[:2]
    dpres = refs[2 : 2 + count]
    gain_ref, shift_ref = refs[2 + count : 4 + count]
    weights = refs[4 + count : 4 + 2 * count]
    dmid_ref, dmid_b_ref, sums_ref = refs[4 + 2 * count :]

    @pl.when(pl.program_id(0) == 0)
    def _():
        sums_ref[...] = jnp.zeros_like(sums_ref)

    dxn = dot(dpres[0][...], weights[0][...], 1, 1)
    for dpre, weight in zip(dpres[1:], weights[1:]):
        dxn = dxn + dot(dpre[...], weight[...], 1, 1)
    gain = gain_ref[...]
    _, normed, scale_inv = norm_forward(mid_ref[...], gain, shift_ref[...])
    gout = gout_ref[...].astype(f32)
    dmid = gout + norm_backward(dxn, normed, scale_inv, gain)
    dmid_ref[...] = dmid
    dmid_b_ref[...] = dmid.astype(bf16)
    for at, value in enumerate((dxn * normed, dxn, dmid, gout)):
        sums_ref[at : at + 1, :] += jnp.sum(value, axis=0, keepdims=True)


def in_back_kernel(count, *refs):
    x_ref, dmid_ref = refs[:2]
    grads = refs[2 : 2 + count]
    gain_ref, shift_ref = refs[2 + count : 4 + count]
    weights = refs[4 + count : 4 + 2 * count]
    out_ref, sums_ref = refs[4 + 2 * count :]

    @pl.when(pl.program_id(0) == 0)
    def _():
        sums_ref[...] = jnp.zeros_like(sums_ref)

    dxn = jnp.zeros(dmid_ref.shape, f32)
    for at in range(count):
        for c in range(3):
            cols = weights[at].shape[2]
            dxn = dxn + dot(grads[at][:, c * cols : (c + 1) * cols], weights[at][c], 1, 1)
    gain = gain_ref[...]
    _, normed, scale_inv = norm_forward(x_ref[...].astype(f32), gain, shift_ref[...])
    out_ref[...] = (dmid_ref[...] + norm_backward(dxn, normed, scale_inv, gain)).astype(bf16)
    for at, value in enumerate((dxn * normed, dxn)):
        sums_ref[at : at + 1, :] += jnp.sum(value, axis=0, keepdims=True)


def local(
    inputs,
    image_count,
    rel_index,
    rel_table,
    norm1_gain,
    norm1_shift,
    w_qkv,
    bias_qv,
    w_proj,
    b_proj,
    norm2_gain,
    norm2_shift,
    w_fc1,
    b_fc1,
    w_fc2,
    b_fc2,
    out_grad,
):
    rows, width = inputs.shape
    window = rel_index.shape[0]
    offsets, heads = rel_table.shape
    shards = lax.axis_size("tensor")
    me = lax.axis_index("tensor")
    head_dim = w_qkv.shape[2] // heads
    scale = head_dim ** (-0.5)
    windows = rows // window
    padded = -(-window // ROW_TILE) * ROW_TILE
    n = windows * padded
    row = lambda value: value.reshape(1, -1)

    def swap(value, bit):
        return lax.ppermute(value, "tensor", [(i, i ^ bit) for i in range(shards)])

    def gather(value):
        got = [value]
        for m in range(1, shards):
            low = m & -m
            got.append(swap(got[m ^ low], low))
        return got

    def pad_rows(value):
        value = value.reshape(windows, window, -1)
        return jnp.pad(value, ((0, 0), (0, padded - window), (0, 0))).reshape(n, -1)

    def cut_rows(value):
        return value.reshape(windows, padded, -1)[:, :window].reshape(rows, -1)

    index = jnp.pad(
        rel_index, ((0, padded - window), (0, padded - window)), constant_values=-1
    )
    onehot = (index[:, :, None] == jnp.arange(offsets, dtype=jnp.int32)).astype(f32)
    bias = jnp.einsum("qkt,th->khq", onehot, rel_table, precision=lax.Precision.HIGHEST)
    keys = jnp.arange(padded, dtype=jnp.int32)[:, None, None]
    bias = jnp.where(keys < window, bias, FAR_BELOW).reshape(padded, heads * padded)

    biases = gather(bias)
    vectors = gather(row(jnp.concatenate([bias_qv.reshape(-1), b_fc1])))
    wqs = gather(w_qkv)
    wps = gather(w_proj)
    w1s = gather(w_fc1)
    w2s = gather(w_fc2)

    row_ids = me * rows + jnp.arange(rows, dtype=jnp.int32)
    live = (row_ids // IMG_TOKENS < image_count[0])[:, None]
    xn1 = norm_forward(inputs.astype(f32), norm1_gain, norm1_shift)[0].astype(bf16)
    xn1 = pad_rows(xn1)
    x_pad = pad_rows(inputs)
    gout = pad_rows(jnp.where(live, out_grad, jnp.zeros_like(out_grad)))

    order = range(shards)
    qkvs, probs, atts = [], [], []
    for m in order:
        qkv, p, att = attend(xn1, wqs[m], vectors[m], biases[m], heads, scale, windows, padded)
        qkvs.append(qkv)
        probs.append(p)
        atts.append(att.reshape(n, -1))

    mid, xn2 = by_rows(
        functools.partial(enter_kernel, shards),
        n,
        [x_pad] + atts,
        [row(b_proj), row(norm2_gain), row(norm2_shift)] + wps,
        [shape_of((n, width)), shape_of((n, width), bf16)],
        [],
        2 * n * width * width,
    )

    ff = w_fc1.shape[1]
    hiddens, dpres, g_b1s, g_fcs = {}, {}, {}, {}
    back_order = list(reversed(order))
    for m in back_order:
        hiddens[m], dpres[m], g_b1s[m], g_fcs[m] = by_rows(
            functools.partial(mlp_kernel, bias_qv.size),
            n,
            [xn2, gout],
            [w1s[m], vectors[m], w2s[m]],
            [shape_of((n, ff), bf16), shape_of((n, ff), bf16)],
            [shape_of((1, ff)), shape_of((2 * ff, width), bf16)],
            8 * n * width * ff,
            [pltpu.VMEM((2 * ff, width), f32)],
        )

    def scatter(parts):
        held = {m: [parts[m]] for m in parts}
        for m in range(shards - 1, 0, -1):
            low = m & -m
            total = held[m][0]
            for term in held[m][1:]:
                total = total + term
            held[m ^ low].append(swap(total, low))
        return held[0]

    groups = lax.axis_size("dp")
    group = lax.axis_index("dp")

    def swap_dp(value, bits):
        return lax.ppermute(value, "dp", [(i, i ^ bits) for i in range(groups)])

    def swap_all(pieces, stride):
        got = []
        for j, piece in enumerate(pieces):
            got.append(swap_dp(piece, j * stride) if j else piece)
        return got

    def sum_dp(terms, ways, results):
        stages = []
        stride = 1
        for way in ways:
            stages.append((stride, way, (group // stride % way).reshape(1)))
            stride *= way
        first = None
        for stride, way, digit in stages:
            pieces = split(terms, digit, way)
            first = pieces[0] if first is None else first
            terms = swap_all(pieces, stride)
        total = terms[0].astype(f32)
        for term in terms[1:]:
            total = total + term.astype(f32)
        total = total.astype(bf16)
        for at, (stride, way, digit) in reversed(list(enumerate(stages))):
            pieces = swap_all([total] * way, stride)
            total = merge(pieces, digit, None if at else results)
        return total, first

    def ways_of(most):
        left = groups
        ways = []
        while left > 1:
            ways.append(min(most[min(len(ways), len(most) - 1)], left))
            left //= ways[-1]
        return ways

    g_fc, _ = sum_dp(scatter(g_fcs), ways_of((4, 2)), [(width, ff), (ff, width)])
    g_fc1, g_fc2 = g_fc

    listed = lambda parts: [parts[m] for m in order]
    dmid, dmid_b, sums2 = by_rows(
        functools.partial(mid_back_kernel, shards),
        n,
        [mid, gout] + listed(dpres),
        [row(norm2_gain), row(norm2_shift)] + w1s,
        [shape_of((n, width)), shape_of((n, width), bf16)],
        [shape_of((8, width))],
        2 * n * width * ff * shards,
    )

    dqkvs, dss, g_bqvs, g_atts = {}, {}, {}, {}
    for m in back_order:
        dqkv, g_atts[m], dss[m], g_bqvs[m] = attend_back(
            dmid_b, xn1, wps[m], qkvs[m], probs[m], atts[m], heads, scale
        )
        dqkvs[m] = dqkv.reshape(n, -1)
    g_att, after_split = sum_dp(scatter(g_atts), ways_of((4, 2)), [w_qkv.shape, w_proj.shape])
    g_qkv, g_proj = g_att

    in_grad, sums1 = by_rows(
        functools.partial(in_back_kernel, shards),
        n,
        [x_pad, dmid] + listed(dqkvs),
        [row(norm1_gain), row(norm1_shift)] + wqs,
        [shape_of((n, width), bf16)],
        [shape_of((8, width))],
        6 * n * width * width,
    )
    (outputs,) = by_rows(
        functools.partial(leave_kernel, shards),
        n,
        [mid] + listed(hiddens),
        [row(b_fc2)] + w2s,
        [shape_of((n, width), bf16)],
        [],
        2 * n * width * ff * shards,
    )
    outputs = cut_rows(outputs)
    outputs = jnp.where(live, outputs, jnp.zeros_like(outputs))
    in_grad = cut_rows(in_grad)

    *late_ds, _ = lax.optimization_barrier((*listed(dss), after_split))
    ds_all = jnp.stack(late_ds).reshape(shards, padded, heads, padded)
    g_tabs = jnp.einsum(
        "qkt,mkhq->mth", onehot, ds_all, precision=lax.Precision.HIGHEST
    )
    per_shard = jnp.concatenate(
        [
            g_tabs.reshape(shards, -1),
            jnp.stack(listed(g_bqvs)).reshape(shards, -1),
            jnp.stack(listed(g_b1s)).reshape(shards, -1),
        ],
        axis=1,
    )
    shared = jnp.concatenate([sums2[:4].reshape(-1), sums1[:2].reshape(-1)])
    per_shard = jnp.concatenate(
        [per_shard, jnp.broadcast_to(shared, (shards, shared.size))], axis=1
    )
    small = sum(scatter({m: per_shard[m] for m in order}))
    bit = 1
    while bit < groups:
        small = small + swap_dp(small, bit)
        bit *= 2
    pieces = []
    at = 0
    for shape in (rel_table.shape, bias_qv.shape, b_fc1.shape) + ((width,),) * 6:
        size = 1
        for extent in shape:
            size *= extent
        pieces.append(small[at : at + size].reshape(shape))
        at += size
    g_tab, g_bqv, g_b_fc1, g_n2g, g_n2s, g_bp, g_b_fc2, g_n1g, g_n1s = pieces
    return (
        outputs,
        in_grad,
        g_tab,
        g_n1g,
        g_n1s,
        g_qkv,
        g_bqv,
        g_proj,
        g_bp,
        g_n2g,
        g_n2s,
        g_fc1,
        g_b_fc1,
        g_fc2,
        g_b_fc2,
    )


def solution(mesh):
    placed = (
        P(("dp", "tensor"), None),
        P("dp"),
        P(),
        P(None, "tensor"),
        P(),
        P(),
        P(None, None, "tensor"),
        P(None, "tensor"),
        P("tensor", None),
        P(),
        P(),
        P(),
        P(None, "tensor"),
        P("tensor"),
        P("tensor", None),
        P(),
        P(("dp", "tensor"), None),
    )
    return jax.shard_map(
        local,
        mesh=mesh,
        in_specs=placed,
        out_specs=(
            P(("dp", "tensor"), None),
            P(("dp", "tensor"), None),
            P(None, "tensor"),
            P(),
            P(),
            P(None, None, "tensor"),
            P(None, "tensor"),
            P("tensor", None),
            P(),
            P(),
            P(),
            P(None, "tensor"),
            P("tensor"),
            P("tensor", None),
            P(),
        ),
        check_vma=False,
    )
```

```python
import functools

import jax
import jax.numpy as jnp
from jax import lax
from jax.experimental import pallas as pl
from jax.experimental.pallas import tpu as pltpu
from jax.sharding import PartitionSpec as P


IMG_TOKENS = 196
ROW_TILE = 16
CHUNK = 512
VMEM_ATTEND = 24 << 20
VMEM_ROWS = 24 << 20
VMEM_MOVE = 16 << 20
TOGETHER = 4
FAR_BELOW = -1e30

eps = 1e-05
f32 = jnp.float32
bf16 = jnp.bfloat16


def norm_forward(values, gain, shift):
    mean = jnp.mean(values, axis=-1, keepdims=True)
    centred = values - mean
    var = jnp.mean(centred * centred, axis=-1, keepdims=True)
    scale_inv = lax.rsqrt(var + eps)
    normed = centred * scale_inv
    return (normed * gain + shift, normed, scale_inv)


def norm_backward(grad, normed, scale_inv, gain):
    scaled = grad * gain
    return scale_inv * (
        scaled
        - jnp.mean(scaled, axis=-1, keepdims=True)
        - normed * jnp.mean(scaled * normed, axis=-1, keepdims=True)
    )


def gelu_parts(pre):
    cdf = 0.5 * (1.0 + lax.erf(pre * 0.7071067811865476))
    dens = jnp.exp(-0.5 * pre * pre) * 0.3989422804014327
    return (pre * cdf, cdf + pre * dens)


def dot(left, right, left_dim, right_dim):
    return lax.dot_general(
        left, right, (((left_dim,), (right_dim,)), ((), ())), preferred_element_type=f32
    )


def head_masks(heads, width):
    head_of = lax.broadcasted_iota(jnp.int32, (1, width), 1) // (width // heads)
    return [(head_of == h).astype(f32) for h in range(heads)]


def spread(value, masks):
    return jnp.concatenate([value * mask.astype(bf16) for mask in masks], axis=0)


def fold(value, masks):
    rows = value.shape[0] // len(masks)
    total = value[:rows] * masks[0]
    for h in range(1, len(masks)):
        total = total + value[h * rows : (h + 1) * rows] * masks[h]
    return total


def together(windows):
    return TOGETHER if windows % TOGETHER == 0 else 1


def blocks(shape, axis=None, size=None):
    if axis is None:
        return pl.BlockSpec(shape, lambda i: (0,) * len(shape))
    block = shape[:axis] + (size,) + shape[axis + 1 :]
    return pl.BlockSpec(block, lambda i: tuple(i if a == axis else 0 for a in range(len(shape))))


def attend_kernel(heads, scale, xn_ref, w_ref, vec_ref, bias_ref, qkv_ref, p_ref, att_ref):
    _, windows, padded, width = qkv_ref.shape
    xn = xn_ref[...]

    def put(c, value):
        qkv_ref[c] = value.astype(bf16).reshape(windows, padded, width)

    put(0, (dot(xn, w_ref[0], 1, 0) + vec_ref[:, :width]) * scale)
    put(1, dot(xn, w_ref[1], 1, 0))
    put(2, dot(xn, w_ref[2], 1, 0) + vec_ref[:, width : 2 * width])
    masks = head_masks(heads, width)

    def some(ws):
        queries = [spread(qkv_ref[0, w], masks) for w in ws]
        scores = [dot(qkv_ref[1, w], q, 1, 1) + bias_ref[...] for w, q in zip(ws, queries)]
        tops = [jnp.max(x, axis=0, keepdims=True) for x in scores]
        powers = [jnp.exp(x - top) for x, top in zip(scores, tops)]
        sums = [jnp.sum(x, axis=0, keepdims=True) for x in powers]
        probs = [x * (1.0 / total) for x, total in zip(powers, sums)]
        outs = [dot(x.astype(bf16), qkv_ref[2, w], 0, 0) for w, x in zip(ws, probs)]
        for w, x, out in zip(ws, probs, outs):
            p_ref[w] = x
            att_ref[w] = fold(out, masks).astype(bf16)

    some(range(windows))


def attend(xn, w, vec, bias, heads, scale, windows, padded):
    width = w.shape[2]
    lanes = heads * padded
    step = together(windows)
    outs = [
        kept((3, windows, padded, width), bf16),
        kept((windows, padded, lanes)),
        kept((windows, padded, width), bf16),
    ]
    return pl.pallas_call(
        functools.partial(attend_kernel, heads, scale),
        grid=(windows // step,),
        in_specs=[
            blocks(xn.shape, 0, step * padded),
            blocks(w.shape),
            blocks(vec.shape),
            blocks(bias.shape),
        ],
        out_specs=[
            blocks(outs[0].shape, 1, step),
            blocks(outs[1].shape, 0, step),
            blocks(outs[2].shape, 0, step),
        ],
        out_shape=outs,
        name="attend",
        compiler_params=pltpu.CompilerParams(vmem_limit_bytes=VMEM_ATTEND),
        cost_estimate=pl.CostEstimate(
            flops=2 * xn.size * 3 * width, bytes_accessed=4 * xn.size, transcendentals=0
        ),
    )(xn, w, vec, bias)


def attend_back_kernel(
    heads,
    scale,
    dmid_ref,
    xn_ref,
    wp_ref,
    qkv_ref,
    p_ref,
    att_ref,
    dqkv_ref,
    g_ref,
    ds_ref,
    gb_ref,
    datt_ref,
    all_ref,
):
    _, windows, padded, width = qkv_ref.shape
    at = pl.program_id(0)
    rows = pl.ds(pl.multiple_of(at * windows * padded, windows * padded), windows * padded)
    datt = dot(dmid_ref[rows, :], wp_ref[...], 1, 1)
    datt_ref[...] = datt.astype(bf16).reshape(windows, padded, width)

    @pl.when(at == 0)
    def _():
        ds_ref[...] = jnp.zeros_like(ds_ref)
        gb_ref[...] = jnp.zeros_like(gb_ref)

    masks = head_masks(heads, width)

    def some(ws):
        probs = [p_ref[w] for w in ws]
        grads = [spread(datt_ref[w], masks) for w in ws]
        dprobs = [dot(qkv_ref[2, w], d, 1, 1) for w, d in zip(ws, grads)]
        dvs = [dot(x.astype(bf16), d, 1, 0) for x, d in zip(probs, grads)]
        inner = [jnp.sum(x * dx, axis=0, keepdims=True) for x, dx in zip(probs, dprobs)]
        dscores = [x * (dx - total) for x, dx, total in zip(probs, dprobs, inner)]
        ds_b = [x.astype(bf16) for x in dscores]
        queries = [spread(qkv_ref[0, w], masks) for w in ws]
        dks = [dot(x, q, 1, 0) for x, q in zip(ds_b, queries)]
        dqs = [fold(dot(x, qkv_ref[1, w], 0, 0), masks) * scale for w, x in zip(ws, ds_b)]
        for w, dq, dk, dv in zip(ws, dqs, dks, dvs):
            dqkv_ref[w] = jnp.concatenate([dq, dk, dv], axis=1).astype(bf16)
        ds_ref[...] += sum(dscores)
        gb_ref[0:1, :] += jnp.sum(sum(dqs), axis=0, keepdims=True)
        gb_ref[1:2, :] += jnp.sum(sum(dvs), axis=0, keepdims=True)

    some(range(windows))
    all_ref[rows, :] = dqkv_ref[...].reshape(windows * padded, 3 * width)

    @pl.when(at == pl.num_programs(0) - 1)
    def _():
        g_ref[:, : 3 * width] = dot(xn_ref[...], all_ref[...], 0, 0).astype(bf16)
        g_ref[:, 3 * width :] = dot(dmid_ref[...], att_ref[...], 0, 0).astype(bf16)


def attend_back(dmid, xn, wp, qkv, probs, att, heads, scale):
    _, windows, padded, width = qkv.shape
    step = together(windows)
    outs = [
        kept((windows, padded, 3 * width), bf16),
        shape_of((dmid.shape[1], 4 * width), bf16),
        shape_of(probs.shape[1:]),
        shape_of((2, width)),
    ]
    return pl.pallas_call(
        functools.partial(attend_back_kernel, heads, scale),
        grid=(windows // step,),
        in_specs=[
            blocks(dmid.shape),
            blocks(xn.shape),
            blocks(wp.shape),
            blocks(qkv.shape, 1, step),
            blocks(probs.shape, 0, step),
            blocks(att.shape),
        ],
        out_specs=[blocks(outs[0].shape, 0, step)] + [blocks(o.shape) for o in outs[1:]],
        out_shape=outs,
        scratch_shapes=[
            pltpu.VMEM((step, padded, width), bf16),
            pltpu.VMEM((windows * padded, 3 * width), bf16),
        ],
        name="attend_back",
        compiler_params=pltpu.CompilerParams(vmem_limit_bytes=VMEM_ATTEND),
        cost_estimate=pl.CostEstimate(
            flops=2 * dmid.size * 8 * width, bytes_accessed=4 * dmid.size, transcendentals=0
        ),
    )(dmid, xn, wp, from_hbm(qkv), from_hbm(probs), att)


def mlp_kernel(
    offset, xn_ref, gout_ref, w1_ref, vec_ref, w2_ref, hidden_ref, dpre_ref, gb_ref, g_ref, sum_ref
):
    ff = w1_ref.shape[1]

    @pl.when(pl.program_id(0) == 0)
    def _():
        gb_ref[...] = jnp.zeros_like(gb_ref)
        sum_ref[...] = jnp.zeros_like(sum_ref)

    xn = xn_ref[...]
    gout = gout_ref[...]
    pre = dot(xn, w1_ref[...], 1, 0) + vec_ref[:, offset:]
    act, slope = gelu_parts(pre)
    hidden = act.astype(bf16)
    hidden_ref[...] = hidden
    dpre = dot(gout, w2_ref[...], 1, 1) * slope
    gb_ref[...] += jnp.sum(dpre, axis=0, keepdims=True)
    dpre_b = dpre.astype(bf16)
    dpre_ref[...] = dpre_b
    sum_ref[:ff] += dot(dpre_b, xn, 0, 0)
    sum_ref[ff:] += dot(hidden, gout, 0, 0)

    @pl.when(pl.program_id(0) == pl.num_programs(0) - 1)
    def _():
        g_ref[...] = sum_ref[...].astype(bf16)


def split_kernel(parts, digit_ref, *refs):
    pieces = refs[parts:]
    rows = pieces[0].shape[0]
    for j, piece in enumerate(pieces):
        start = pl.multiple_of((digit_ref[0] ^ j) * rows, rows)
        total = refs[0][pl.ds(start, rows), :].astype(f32)
        for ref in refs[1:parts]:
            total = total + ref[pl.ds(start, rows), :].astype(f32)
        piece[...] = total.astype(bf16)


def split(values, digit, ways):
    rows, width = values[0].shape
    return pl.pallas_call(
        functools.partial(split_kernel, len(values)),
        in_specs=[pl.BlockSpec(memory_space=pltpu.SMEM)]
        + [pl.BlockSpec(memory_space=pltpu.VMEM)] * len(values),
        out_shape=[shape_of((rows // ways, width), bf16)] * ways,
        name="split",
        compiler_params=pltpu.CompilerParams(vmem_limit_bytes=VMEM_MOVE),
    )(digit, *values)


def merge_kernel(ways, digit_ref, *refs):
    out_ref = refs[-1]
    rows = refs[0].shape[0]
    for j in range(ways):
        start = pl.multiple_of((digit_ref[0] ^ j) * rows, rows)
        out_ref[pl.ds(start, rows), :] = refs[j][...].astype(out_ref.dtype)
    if len(refs) == ways + 1:
        return
    first, second = refs[ways : ways + 2]
    if len(first.shape) == 3:
        cols = first.shape[2]
        for c in range(3):
            first[c] = out_ref[:, c * cols : (c + 1) * cols]
        second[...] = out_ref[:, 3 * cols :].T
    else:
        ff = second.shape[0]
        first[...] = out_ref[:ff, :].T
        second[...] = out_ref[ff:, :]


def merge(pieces, digit, results):
    ways = len(pieces)
    rows, width = pieces[0].shape
    whole = (rows * ways, width)
    return pl.pallas_call(
        functools.partial(merge_kernel, ways),
        in_specs=[pl.BlockSpec(memory_space=pltpu.SMEM)]
        + [pl.BlockSpec(memory_space=pltpu.VMEM)] * ways,
        out_shape=[shape_of(r) for r in results] if results else shape_of(whole, bf16),
        scratch_shapes=[pltpu.VMEM(whole, f32)] if results else [],
        name="merge",
        compiler_params=pltpu.CompilerParams(vmem_limit_bytes=VMEM_MOVE),
    )(digit, *pieces)


def by_rows(kernel, rows, cut, whole, cut_outs, whole_outs, flops, scratch=(), chunk=CHUNK):
    chunk = chunk if rows % chunk == 0 else rows

    def cut_spec(value):
        return pl.BlockSpec((chunk,) + value.shape[1:], lambda i: (i,) + (0,) * (len(value.shape) - 1))

    def whole_spec(value):
        return pl.BlockSpec(value.shape, lambda i: (0,) * len(value.shape))

    return pl.pallas_call(
        kernel,
        grid=(rows // chunk,),
        in_specs=[cut_spec(v) for v in cut] + [whole_spec(v) for v in whole],
        out_specs=[cut_spec(v) for v in cut_outs] + [whole_spec(v) for v in whole_outs],
        out_shape=list(cut_outs) + list(whole_outs),
        scratch_shapes=list(scratch),
        compiler_params=pltpu.CompilerParams(vmem_limit_bytes=VMEM_ROWS),
        cost_estimate=pl.CostEstimate(
            flops=flops,
            bytes_accessed=sum(v.size * v.dtype.itemsize for v in cut),
            transcendentals=0,
        ),
    )(*cut, *whole)


def shape_of(shape, dtype=f32):
    return jax.ShapeDtypeStruct(shape, dtype)


def kept(shape, dtype=f32):
    return pltpu.HBM(shape, dtype)


def from_hbm(value):
    return pltpu.with_memory_space_constraint(value, pltpu.HBM)


def prepare_kernel(
    window, live_ref, x_ref, grad_ref, gain_ref, shift_ref, pad_ref, xn_ref, gout_ref, xs_ref, gs_ref
):
    rows = x_ref.shape[0]
    windows, padded, _ = pad_ref.shape
    live = lax.broadcasted_iota(jnp.int32, (rows, 1), 0) < live_ref[0]
    xs_ref[:rows, :] = x_ref[...].astype(f32)
    gs_ref[:rows, :] = jnp.where(live, grad_ref[...].astype(f32), 0.0)
    xs_ref[rows:, :] = jnp.zeros_like(xs_ref[rows:, :])
    gs_ref[rows:, :] = jnp.zeros_like(gs_ref[rows:, :])
    real = lax.broadcasted_iota(jnp.int32, (padded, 1), 0) < window
    gain = gain_ref[...]
    shift = shift_ref[...]
    for w in range(windows):
        taken = slice(w * window, w * window + padded)
        values = xs_ref[taken, :]
        pad_ref[w] = jnp.where(real, values, 0.0).astype(bf16)
        xn_ref[w] = jnp.where(real, norm_forward(values, gain, shift)[0], 0.0).astype(bf16)
        gout_ref[w] = jnp.where(real, gs_ref[taken, :], 0.0).astype(bf16)


def prepare(live, x, grad, gain, shift, window, padded):
    rows, width = x.shape
    shape = (rows // window, padded, width)
    held = -(-(rows - window + padded) // ROW_TILE) * ROW_TILE
    outs = pl.pallas_call(
        functools.partial(prepare_kernel, window),
        in_specs=[pl.BlockSpec(memory_space=pltpu.SMEM)]
        + [pl.BlockSpec(memory_space=pltpu.VMEM)] * 4,
        out_shape=[shape_of(shape, bf16)] * 3,
        scratch_shapes=[pltpu.VMEM((held, width), f32)] * 2,
        name="prepare",
        compiler_params=pltpu.CompilerParams(vmem_limit_bytes=VMEM_ROWS),
    )(live.reshape(1), x, grad, gain, shift)
    return [out.reshape(-1, width) for out in outs]


def enter_kernel(count, *refs):
    x_ref, atts = refs[0], refs[1 : 1 + count]
    b_ref, gain_ref, shift_ref = refs[1 + count : 4 + count]
    weights = refs[4 + count : 4 + 2 * count]
    mid_ref, xn_ref = refs[4 + 2 * count :]
    total = dot(atts[0][...], weights[0][...], 1, 0)
    for att, weight in zip(atts[1:], weights[1:]):
        total = total + dot(att[...], weight[...], 1, 0)
    mid = x_ref[...].astype(f32) + (total + b_ref[...])
    mid_ref[...] = mid
    xn_ref[...] = norm_forward(mid, gain_ref[...], shift_ref[...])[0].astype(bf16)


def leave_kernel(count, *refs):
    mid_ref, hiddens = refs[0], refs[1 : 1 + count]
    b_ref, weights = refs[1 + count], refs[2 + count : 2 + 2 * count]
    out_ref = refs[2 + 2 * count]
    total = dot(hiddens[0][...], weights[0][...], 1, 0)
    for hidden, weight in zip(hiddens[1:], weights[1:]):
        total = total + dot(hidden[...], weight[...], 1, 0)
    out_ref[...] = (mid_ref[...] + total + b_ref[...]).astype(bf16)


def mid_back_kernel(count, *refs):
    mid_ref, gout_ref = refs[:2]
    dpres = refs[2 : 2 + count]
    gain_ref, shift_ref = refs[2 + count : 4 + count]
    weights = refs[4 + count : 4 + 2 * count]
    dmid_ref, dmid_b_ref, sums_ref = refs[4 + 2 * count :]

    @pl.when(pl.program_id(0) == 0)
    def _():
        sums_ref[...] = jnp.zeros_like(sums_ref)

    dxn = dot(dpres[0][...], weights[0][...], 1, 1)
    for dpre, weight in zip(dpres[1:], weights[1:]):
        dxn = dxn + dot(dpre[...], weight[...], 1, 1)
    gain = gain_ref[...]
    _, normed, scale_inv = norm_forward(mid_ref[...], gain, shift_ref[...])
    gout = gout_ref[...].astype(f32)
    dmid = gout + norm_backward(dxn, normed, scale_inv, gain)
    dmid_ref[...] = dmid
    dmid_b_ref[...] = dmid.astype(bf16)
    for at, value in enumerate((dxn * normed, dxn, dmid, gout)):
        sums_ref[at : at + 1, :] += jnp.sum(value, axis=0, keepdims=True)


def in_back_kernel(count, *refs):
    x_ref, dmid_ref = refs[:2]
    grads = refs[2 : 2 + count]
    gain_ref, shift_ref = refs[2 + count : 4 + count]
    weights = refs[4 + count : 4 + 2 * count]
    out_ref, sums_ref = refs[4 + 2 * count :]

    @pl.when(pl.program_id(0) == 0)
    def _():
        sums_ref[...] = jnp.zeros_like(sums_ref)

    dxn = jnp.zeros(dmid_ref.shape, f32)
    for at in range(count):
        for c in range(3):
            cols = weights[at].shape[2]
            dxn = dxn + dot(grads[at][:, c * cols : (c + 1) * cols], weights[at][c], 1, 1)
    gain = gain_ref[...]
    _, normed, scale_inv = norm_forward(x_ref[...].astype(f32), gain, shift_ref[...])
    out_ref[...] = (dmid_ref[...] + norm_backward(dxn, normed, scale_inv, gain)).astype(bf16)
    for at, value in enumerate((dxn * normed, dxn)):
        sums_ref[at : at + 1, :] += jnp.sum(value, axis=0, keepdims=True)


def local(
    inputs,
    image_count,
    rel_index,
    rel_table,
    norm1_gain,
    norm1_shift,
    w_qkv,
    bias_qv,
    w_proj,
    b_proj,
    norm2_gain,
    norm2_shift,
    w_fc1,
    b_fc1,
    w_fc2,
    b_fc2,
    out_grad,
):
    rows, width = inputs.shape
    window = rel_index.shape[0]
    offsets, heads = rel_table.shape
    shards = lax.axis_size("tensor")
    me = lax.axis_index("tensor")
    head_dim = w_qkv.shape[2] // heads
    scale = head_dim ** (-0.5)
    windows = rows // window
    padded = -(-window // ROW_TILE) * ROW_TILE
    n = windows * padded
    row = lambda value: value.reshape(1, -1)

    def swap(value, bit):
        return lax.ppermute(value, "tensor", [(i, i ^ bit) for i in range(shards)])

    def gather(value):
        got = [value]
        for m in range(1, shards):
            low = m & -m
            got.append(swap(got[m ^ low], low))
        return got

    def cut_rows(value):
        return value.reshape(windows, padded, -1)[:, :window].reshape(rows, -1)

    index = jnp.pad(
        rel_index, ((0, padded - window), (0, padded - window)), constant_values=-1
    )
    onehot = (index[:, :, None] == jnp.arange(offsets, dtype=jnp.int32)).astype(f32)
    bias = jnp.einsum("qkt,th->khq", onehot, rel_table, precision=lax.Precision.HIGHEST)
    keys = jnp.arange(padded, dtype=jnp.int32)[:, None, None]
    bias = jnp.where(keys < window, bias, FAR_BELOW).reshape(padded, heads * padded)

    biases = gather(bias)
    vectors = gather(row(jnp.concatenate([bias_qv.reshape(-1), b_fc1])))
    wqs = gather(w_qkv)
    wps = gather(w_proj)
    w1s = gather(w_fc1)
    w2s = gather(w_fc2)

    live_rows = image_count[0] * IMG_TOKENS - me * rows
    live = (jnp.arange(rows, dtype=jnp.int32) < live_rows)[:, None]
    x_pad, xn1, gout = prepare(
        live_rows, inputs, out_grad, row(norm1_gain), row(norm1_shift), window, padded
    )

    order = range(shards)
    qkvs, probs, atts = [], [], []
    for m in order:
        qkv, p, att = attend(xn1, wqs[m], vectors[m], biases[m], heads, scale, windows, padded)
        qkvs.append(qkv)
        probs.append(p)
        atts.append(att.reshape(n, -1))

    mid, xn2 = by_rows(
        functools.partial(enter_kernel, shards),
        n,
        [from_hbm(v) for v in [x_pad] + atts],
        [row(b_proj), row(norm2_gain), row(norm2_shift)] + wps,
        [kept((n, width)), shape_of((n, width), bf16)],
        [],
        2 * n * width * width,
    )

    ff = w_fc1.shape[1]
    hiddens, dpres, g_b1s, g_fcs = {}, {}, {}, {}
    back_order = list(reversed(order))
    for m in mlp_order(shards):
        hiddens[m], dpres[m], g_b1s[m], g_fcs[m] = by_rows(
            functools.partial(mlp_kernel, bias_qv.size),
            n,
            [xn2, gout],
            [w1s[m], vectors[m], w2s[m]],
            [kept((n, ff), bf16), kept((n, ff), bf16)],
            [shape_of((1, ff)), shape_of((2 * ff, width), bf16)],
            8 * n * width * ff,
            [pltpu.VMEM((2 * ff, width), f32)],
            n,
        )

    def scatter(parts):
        held = {m: [parts[m]] for m in parts}
        for m in range(shards - 1, 0, -1):
            low = m & -m
            total = held[m][0]
            for term in held[m][1:]:
                total = total + term
            held[m ^ low].append(swap(total, low))
        return held[0]

    groups = lax.axis_size("dp")
    group = lax.axis_index("dp")

    def swap_dp(value, bits):
        return lax.ppermute(value, "dp", [(i, i ^ bits) for i in range(groups)])

    def swap_all(pieces, stride):
        got = []
        for j, piece in enumerate(pieces):
            got.append(swap_dp(piece, j * stride) if j else piece)
        return got

    def sum_dp(terms, ways, results):
        stages = []
        stride = 1
        for way in ways:
            stages.append((stride, way, (group // stride % way).reshape(1)))
            stride *= way
        first = None
        for stride, way, digit in stages:
            pieces = split(terms, digit, way)
            first = pieces[0] if first is None else first
            terms = swap_all(pieces, stride)
        total = terms[0].astype(f32)
        for term in terms[1:]:
            total = total + term.astype(f32)
        total = total.astype(bf16)
        for at, (stride, way, digit) in reversed(list(enumerate(stages))):
            pieces = swap_all([total] * way, stride)
            total = merge(pieces, digit, None if at else results)
        return total, first

    def ways_of(most):
        left = groups
        ways = []
        while left > 1:
            ways.append(min(most[min(len(ways), len(most) - 1)], left))
            left //= ways[-1]
        return ways

    g_fc, _ = sum_dp(scatter(g_fcs), ways_of((4, 2)), [(width, ff), (ff, width)])
    g_fc1, g_fc2 = g_fc

    listed = lambda parts: [parts[m] for m in order]
    dmid, dmid_b, sums2 = by_rows(
        functools.partial(mid_back_kernel, shards),
        n,
        [from_hbm(v) for v in [mid, gout] + listed(dpres)],
        [row(norm2_gain), row(norm2_shift)] + w1s,
        [kept((n, width)), shape_of((n, width), bf16)],
        [shape_of((8, width))],
        2 * n * width * ff * shards,
    )

    dqkvs, dss, g_bqvs, g_atts = {}, {}, {}, {}
    for m in back_order:
        dqkv, g_atts[m], dss[m], g_bqvs[m] = attend_back(
            dmid_b, xn1, wps[m], qkvs[m], probs[m], atts[m], heads, scale
        )
        dqkvs[m] = dqkv.reshape(n, -1)
    g_att, after_split = sum_dp(scatter(g_atts), ways_of((4, 2)), [w_qkv.shape, w_proj.shape])
    g_qkv, g_proj = g_att

    in_grad, sums1 = by_rows(
        functools.partial(in_back_kernel, shards),
        n,
        [from_hbm(v) for v in [x_pad, dmid] + listed(dqkvs)],
        [row(norm1_gain), row(norm1_shift)] + wqs,
        [shape_of((n, width), bf16)],
        [shape_of((8, width))],
        6 * n * width * width,
    )
    (outputs,) = by_rows(
        functools.partial(leave_kernel, shards),
        n,
        [from_hbm(v) for v in [mid] + listed(hiddens)],
        [row(b_fc2)] + w2s,
        [shape_of((n, width), bf16)],
        [],
        2 * n * width * ff * shards,
    )
    outputs = cut_rows(outputs)
    outputs = jnp.where(live, outputs, jnp.zeros_like(outputs))
    in_grad = cut_rows(in_grad)

    *late_ds, _ = lax.optimization_barrier((*listed(dss), after_split))
    ds_all = jnp.stack(late_ds).reshape(shards, padded, heads, padded)
    g_tabs = jnp.einsum(
        "qkt,mkhq->mth", onehot, ds_all, precision=lax.Precision.HIGHEST
    )
    per_shard = jnp.concatenate(
        [
            g_tabs.reshape(shards, -1),
            jnp.stack(listed(g_bqvs)).reshape(shards, -1),
            jnp.stack(listed(g_b1s)).reshape(shards, -1),
        ],
        axis=1,
    )
    shared = jnp.concatenate([sums2[:4].reshape(-1), sums1[:2].reshape(-1)])
    per_shard = jnp.concatenate(
        [per_shard, jnp.broadcast_to(shared, (shards, shared.size))], axis=1
    )
    small = sum(scatter({m: per_shard[m] for m in order}))
    bit = 1
    while bit < groups:
        small = small + swap_dp(small, bit)
        bit *= 2
    pieces = []
    at = 0
    for shape in (rel_table.shape, bias_qv.shape, b_fc1.shape) + ((width,),) * 6:
        size = 1
        for extent in shape:
            size *= extent
        pieces.append(small[at : at + size].reshape(shape))
        at += size
    g_tab, g_bqv, g_b_fc1, g_n2g, g_n2s, g_bp, g_b_fc2, g_n1g, g_n1s = pieces
    return (
        outputs,
        in_grad,
        g_tab,
        g_n1g,
        g_n1s,
        g_qkv,
        g_bqv,
        g_proj,
        g_bp,
        g_n2g,
        g_n2s,
        g_fc1,
        g_b_fc1,
        g_fc2,
        g_b_fc2,
    )


def mlp_order(shards):
    return [1] * (shards > 1) + [m for m in range(shards - 1, -1, -1) if m != 1]


def solution(mesh):
    placed = (
        P(("dp", "tensor"), None),
        P("dp"),
        P(),
        P(None, "tensor"),
        P(),
        P(),
        P(None, None, "tensor"),
        P(None, "tensor"),
        P("tensor", None),
        P(),
        P(),
        P(),
        P(None, "tensor"),
        P("tensor"),
        P("tensor", None),
        P(),
        P(("dp", "tensor"), None),
    )
    return jax.shard_map(
        local,
        mesh=mesh,
        in_specs=placed,
        out_specs=(
            P(("dp", "tensor"), None),
            P(("dp", "tensor"), None),
            P(None, "tensor"),
            P(),
            P(),
            P(None, None, "tensor"),
            P(None, "tensor"),
            P("tensor", None),
            P(),
            P(),
            P(),
            P(None, "tensor"),
            P("tensor"),
            P("tensor", None),
            P(),
        ),
        check_vma=False,
    )
```

```python
import functools

import jax
import jax.numpy as jnp
from jax import lax
from jax.experimental import pallas as pl
from jax.experimental.pallas import tpu as pltpu
from jax.sharding import PartitionSpec as P


IMG_TOKENS = 196
ROW_TILE = 16
CHUNK = 512
VMEM_ATTEND = 24 << 20
VMEM_ROWS = 24 << 20
VMEM_MOVE = 16 << 20
TOGETHER = 16
FAR_BELOW = -1e30

TENSOR = "tensor"
DP = "dp"

eps = 1e-05
f32 = jnp.float32
bf16 = jnp.bfloat16


def norm_forward(values, gain, shift):
    mean = jnp.mean(values, axis=-1, keepdims=True)
    centred = values - mean
    var = jnp.mean(centred * centred, axis=-1, keepdims=True)
    scale_inv = lax.rsqrt(var + eps)
    normed = centred * scale_inv
    return (normed * gain + shift, normed, scale_inv)


def norm_backward(grad, normed, scale_inv, gain):
    scaled = grad * gain
    return scale_inv * (
        scaled
        - jnp.mean(scaled, axis=-1, keepdims=True)
        - normed * jnp.mean(scaled * normed, axis=-1, keepdims=True)
    )


def gelu_parts(pre):
    cdf = 0.5 * (1.0 + lax.erf(pre * 0.7071067811865476))
    dens = jnp.exp(-0.5 * pre * pre) * 0.3989422804014327
    return (pre * cdf, cdf + pre * dens)


def dot(left, right, left_dim, right_dim):
    return lax.dot_general(
        left, right, (((left_dim,), (right_dim,)), ((), ())), preferred_element_type=f32
    )


def head_masks(heads, width):
    head_of = lax.broadcasted_iota(jnp.int32, (1, width), 1) // (width // heads)
    return [(head_of == h).astype(f32) for h in range(heads)]


def spread(value, masks):
    return jnp.concatenate([value * mask.astype(bf16) for mask in masks], axis=0)


def fold(value, masks):
    rows = value.shape[0] // len(masks)
    total = value[:rows] * masks[0]
    for h in range(1, len(masks)):
        total = total + value[h * rows : (h + 1) * rows] * masks[h]
    return total


def together(windows):
    return max(size for size in range(1, TOGETHER + 1) if windows % size == 0)


def blocks(shape, axis=None, size=None):
    if axis is None:
        return pl.BlockSpec(shape, lambda i: (0,) * len(shape))
    block = shape[:axis] + (size,) + shape[axis + 1 :]
    return pl.BlockSpec(block, lambda i: tuple(i if a == axis else 0 for a in range(len(shape))))


def attend_kernel(heads, scale, xn_ref, w_ref, vec_ref, bias_ref, qkv_ref, p_ref, att_ref):
    _, windows, padded, width = qkv_ref.shape
    xn = xn_ref[...]

    def put(c, value):
        qkv_ref[c] = value.astype(bf16).reshape(windows, padded, width)

    put(0, (dot(xn, w_ref[0], 1, 0) + vec_ref[:, :width]) * scale)
    put(1, dot(xn, w_ref[1], 1, 0))
    put(2, dot(xn, w_ref[2], 1, 0) + vec_ref[:, width : 2 * width])
    masks = head_masks(heads, width)

    def some(ws):
        queries = [spread(qkv_ref[0, w], masks) for w in ws]
        scores = [dot(qkv_ref[1, w], q, 1, 1) + bias_ref[...] for w, q in zip(ws, queries)]
        tops = [jnp.max(x, axis=0, keepdims=True) for x in scores]
        powers = [jnp.exp(x - top) for x, top in zip(scores, tops)]
        sums = [jnp.sum(x, axis=0, keepdims=True) for x in powers]
        probs = [x * (1.0 / total) for x, total in zip(powers, sums)]
        outs = [dot(x.astype(bf16), qkv_ref[2, w], 0, 0) for w, x in zip(ws, probs)]
        for w, x, out in zip(ws, probs, outs):
            p_ref[w] = x
            att_ref[w] = fold(out, masks).astype(bf16)

    some(range(windows))


def attend(xn, w, vec, bias, heads, scale, windows, padded):
    width = w.shape[2]
    lanes = heads * padded
    step = together(windows)
    outs = [
        kept((3, windows, padded, width), bf16),
        kept((windows, padded, lanes)),
        kept((windows, padded, width), bf16),
    ]
    return pl.pallas_call(
        functools.partial(attend_kernel, heads, scale),
        grid=(windows // step,),
        in_specs=[
            blocks(xn.shape, 0, step * padded),
            blocks(w.shape),
            blocks(vec.shape),
            blocks(bias.shape),
        ],
        out_specs=[
            blocks(outs[0].shape, 1, step),
            blocks(outs[1].shape, 0, step),
            blocks(outs[2].shape, 0, step),
        ],
        out_shape=outs,
        name="attend",
        compiler_params=pltpu.CompilerParams(vmem_limit_bytes=VMEM_ATTEND),
        cost_estimate=pl.CostEstimate(
            flops=2 * xn.size * 3 * width, bytes_accessed=4 * xn.size, transcendentals=0
        ),
    )(xn, w, vec, bias)


def attend_back_kernel(
    heads,
    scale,
    dmid_ref,
    xn_ref,
    wp_ref,
    qkv_ref,
    p_ref,
    att_ref,
    dqkv_ref,
    g_ref,
    ds_ref,
    gb_ref,
    datt_ref,
    all_ref,
):
    _, windows, padded, width = qkv_ref.shape
    at = pl.program_id(0)
    rows = pl.ds(pl.multiple_of(at * windows * padded, windows * padded), windows * padded)
    datt = dot(dmid_ref[rows, :], wp_ref[...], 1, 1)
    datt_ref[...] = datt.astype(bf16).reshape(windows, padded, width)

    @pl.when(at == 0)
    def _():
        ds_ref[...] = jnp.zeros_like(ds_ref)
        gb_ref[...] = jnp.zeros_like(gb_ref)

    masks = head_masks(heads, width)

    def some(ws):
        probs = [p_ref[w] for w in ws]
        grads = [spread(datt_ref[w], masks) for w in ws]
        dprobs = [dot(qkv_ref[2, w], d, 1, 1) for w, d in zip(ws, grads)]
        dvs = [dot(x.astype(bf16), d, 1, 0) for x, d in zip(probs, grads)]
        inner = [jnp.sum(x * dx, axis=0, keepdims=True) for x, dx in zip(probs, dprobs)]
        dscores = [x * (dx - total) for x, dx, total in zip(probs, dprobs, inner)]
        ds_b = [x.astype(bf16) for x in dscores]
        queries = [spread(qkv_ref[0, w], masks) for w in ws]
        dks = [dot(x, q, 1, 0) for x, q in zip(ds_b, queries)]
        dqs = [fold(dot(x, qkv_ref[1, w], 0, 0), masks) * scale for w, x in zip(ws, ds_b)]
        for w, dq, dk, dv in zip(ws, dqs, dks, dvs):
            dqkv_ref[w] = jnp.concatenate([dq, dk, dv], axis=1).astype(bf16)
        ds_ref[...] += sum(dscores)
        gb_ref[0:1, :] += jnp.sum(sum(dqs), axis=0, keepdims=True)
        gb_ref[1:2, :] += jnp.sum(sum(dvs), axis=0, keepdims=True)

    some(range(windows))
    all_ref[rows, :] = dqkv_ref[...].reshape(windows * padded, 3 * width)

    @pl.when(at == pl.num_programs(0) - 1)
    def _():
        g_ref[:, : 3 * width] = dot(xn_ref[...], all_ref[...], 0, 0).astype(bf16)
        g_ref[:, 3 * width :] = dot(dmid_ref[...], att_ref[...], 0, 0).astype(bf16)


def attend_back(dmid, xn, wp, qkv, probs, att, heads, scale):
    _, windows, padded, width = qkv.shape
    step = together(windows)
    outs = [
        kept((windows, padded, 3 * width), bf16),
        shape_of((dmid.shape[1], 4 * width), bf16),
        shape_of(probs.shape[1:]),
        shape_of((2, width)),
    ]
    return pl.pallas_call(
        functools.partial(attend_back_kernel, heads, scale),
        grid=(windows // step,),
        in_specs=[
            blocks(dmid.shape),
            blocks(xn.shape),
            blocks(wp.shape),
            blocks(qkv.shape, 1, step),
            blocks(probs.shape, 0, step),
            blocks(att.shape),
        ],
        out_specs=[blocks(outs[0].shape, 0, step)] + [blocks(o.shape) for o in outs[1:]],
        out_shape=outs,
        scratch_shapes=[
            pltpu.VMEM((step, padded, width), bf16),
            pltpu.VMEM((windows * padded, 3 * width), bf16),
        ],
        name="back",
        compiler_params=pltpu.CompilerParams(vmem_limit_bytes=VMEM_ATTEND),
        cost_estimate=pl.CostEstimate(
            flops=2 * dmid.size * 8 * width, bytes_accessed=4 * dmid.size, transcendentals=0
        ),
    )(dmid, xn, wp, from_hbm(qkv), from_hbm(probs), att)


def mlp_kernel(
    offset, xn_ref, gout_ref, w1_ref, vec_ref, w2_ref, hidden_ref, dpre_ref, gb_ref, g_ref, sum_ref
):
    ff = w1_ref.shape[1]

    @pl.when(pl.program_id(0) == 0)
    def _():
        gb_ref[...] = jnp.zeros_like(gb_ref)
        sum_ref[...] = jnp.zeros_like(sum_ref)

    xn = xn_ref[...]
    gout = gout_ref[...]
    pre = dot(xn, w1_ref[...], 1, 0) + vec_ref[:, offset:]
    act, slope = gelu_parts(pre)
    hidden = act.astype(bf16)
    hidden_ref[...] = hidden
    dpre = dot(gout, w2_ref[...], 1, 1) * slope
    gb_ref[...] += jnp.sum(dpre, axis=0, keepdims=True)
    dpre_b = dpre.astype(bf16)
    dpre_ref[...] = dpre_b
    sum_ref[:ff] += dot(dpre_b, xn, 0, 0)
    sum_ref[ff:] += dot(hidden, gout, 0, 0)

    @pl.when(pl.program_id(0) == pl.num_programs(0) - 1)
    def _():
        g_ref[...] = sum_ref[...].astype(bf16)


def split_kernel(parts, digit_ref, *refs):
    pieces = refs[parts:]
    rows = pieces[0].shape[0]
    for j, piece in enumerate(pieces):
        start = pl.multiple_of((digit_ref[0] ^ j) * rows, rows)
        total = refs[0][pl.ds(start, rows), :].astype(f32)
        for ref in refs[1:parts]:
            total = total + ref[pl.ds(start, rows), :].astype(f32)
        piece[...] = total.astype(bf16)


def split(values, digit, ways):
    rows, width = values[0].shape
    return pl.pallas_call(
        functools.partial(split_kernel, len(values)),
        in_specs=[pl.BlockSpec(memory_space=pltpu.SMEM)]
        + [pl.BlockSpec(memory_space=pltpu.VMEM)] * len(values),
        out_shape=[shape_of((rows // ways, width), bf16)] * ways,
        name="split",
        compiler_params=pltpu.CompilerParams(vmem_limit_bytes=VMEM_MOVE),
    )(digit, *values)


def merge_kernel(ways, digit_ref, *refs):
    out_ref = refs[-1]
    rows = refs[0].shape[0]
    for j in range(ways):
        start = pl.multiple_of((digit_ref[0] ^ j) * rows, rows)
        out_ref[pl.ds(start, rows), :] = refs[j][...].astype(out_ref.dtype)
    if len(refs) == ways + 1:
        return
    first, second = refs[ways : ways + 2]
    if len(first.shape) == 3:
        cols = first.shape[2]
        for c in range(3):
            first[c] = out_ref[:, c * cols : (c + 1) * cols]
        second[...] = out_ref[:, 3 * cols :].T
    else:
        ff = second.shape[0]
        first[...] = out_ref[:ff, :].T
        second[...] = out_ref[ff:, :]


def merge(pieces, digit, results):
    ways = len(pieces)
    rows, width = pieces[0].shape
    whole = (rows * ways, width)
    return pl.pallas_call(
        functools.partial(merge_kernel, ways),
        in_specs=[pl.BlockSpec(memory_space=pltpu.SMEM)]
        + [pl.BlockSpec(memory_space=pltpu.VMEM)] * ways,
        out_shape=[shape_of(r) for r in results] if results else shape_of(whole, bf16),
        scratch_shapes=[pltpu.VMEM(whole, f32)] if results else [],
        name="merge",
        compiler_params=pltpu.CompilerParams(vmem_limit_bytes=VMEM_MOVE),
    )(digit, *pieces)


def by_rows(kernel, rows, cut, whole, cut_outs, whole_outs, flops, scratch=(), chunk=CHUNK):
    chunk = chunk if rows % chunk == 0 else rows

    def cut_spec(value):
        return pl.BlockSpec((chunk,) + value.shape[1:], lambda i: (i,) + (0,) * (len(value.shape) - 1))

    def whole_spec(value):
        return pl.BlockSpec(value.shape, lambda i: (0,) * len(value.shape))

    return pl.pallas_call(
        kernel,
        grid=(rows // chunk,),
        in_specs=[cut_spec(v) for v in cut] + [whole_spec(v) for v in whole],
        out_specs=[cut_spec(v) for v in cut_outs] + [whole_spec(v) for v in whole_outs],
        out_shape=list(cut_outs) + list(whole_outs),
        scratch_shapes=list(scratch),
        compiler_params=pltpu.CompilerParams(vmem_limit_bytes=VMEM_ROWS),
        cost_estimate=pl.CostEstimate(
            flops=flops,
            bytes_accessed=sum(v.size * v.dtype.itemsize for v in cut),
            transcendentals=0,
        ),
    )(*cut, *whole)


def shape_of(shape, dtype=f32):
    return jax.ShapeDtypeStruct(shape, dtype)


def kept(shape, dtype=f32):
    return pltpu.HBM(shape, dtype)


def from_hbm(value):
    return pltpu.with_memory_space_constraint(value, pltpu.HBM)


def prepare_kernel(
    window, live_ref, x_ref, grad_ref, gain_ref, shift_ref, pad_ref, xn_ref, gout_ref, xs_ref, gs_ref
):
    rows = x_ref.shape[0]
    windows, padded, _ = pad_ref.shape
    live = lax.broadcasted_iota(jnp.int32, (rows, 1), 0) < live_ref[0]
    xs_ref[:rows, :] = x_ref[...].astype(f32)
    gs_ref[:rows, :] = jnp.where(live, grad_ref[...].astype(f32), 0.0)
    xs_ref[rows:, :] = jnp.zeros_like(xs_ref[rows:, :])
    gs_ref[rows:, :] = jnp.zeros_like(gs_ref[rows:, :])
    real = lax.broadcasted_iota(jnp.int32, (padded, 1), 0) < window
    gain = gain_ref[...]
    shift = shift_ref[...]
    for w in range(windows):
        taken = slice(w * window, w * window + padded)
        values = xs_ref[taken, :]
        pad_ref[w] = jnp.where(real, values, 0.0).astype(bf16)
        xn_ref[w] = jnp.where(real, norm_forward(values, gain, shift)[0], 0.0).astype(bf16)
        gout_ref[w] = jnp.where(real, gs_ref[taken, :], 0.0).astype(bf16)


def prepare(live, x, grad, gain, shift, window, padded):
    rows, width = x.shape
    shape = (rows // window, padded, width)
    held = -(-(rows - window + padded) // ROW_TILE) * ROW_TILE
    outs = pl.pallas_call(
        functools.partial(prepare_kernel, window),
        in_specs=[pl.BlockSpec(memory_space=pltpu.SMEM)]
        + [pl.BlockSpec(memory_space=pltpu.VMEM)] * 4,
        out_shape=[shape_of(shape, bf16)] * 3,
        scratch_shapes=[pltpu.VMEM((held, width), f32)] * 2,
        name="prepare",
        compiler_params=pltpu.CompilerParams(vmem_limit_bytes=VMEM_ROWS),
    )(live.reshape(1), x, grad, gain, shift)
    return [out.reshape(-1, width) for out in outs]


def enter_kernel(count, *refs):
    x_ref, atts = refs[0], refs[1 : 1 + count]
    b_ref, gain_ref, shift_ref = refs[1 + count : 4 + count]
    weights = refs[4 + count : 4 + 2 * count]
    mid_ref, xn_ref = refs[4 + 2 * count :]
    total = dot(atts[0][...], weights[0][...], 1, 0)
    for att, weight in zip(atts[1:], weights[1:]):
        total = total + dot(att[...], weight[...], 1, 0)
    mid = x_ref[...].astype(f32) + (total + b_ref[...])
    mid_ref[...] = mid
    xn_ref[...] = norm_forward(mid, gain_ref[...], shift_ref[...])[0].astype(bf16)


def leave_kernel(count, *refs):
    mid_ref, hiddens = refs[0], refs[1 : 1 + count]
    b_ref, weights = refs[1 + count], refs[2 + count : 2 + 2 * count]
    out_ref = refs[2 + 2 * count]
    total = dot(hiddens[0][...], weights[0][...], 1, 0)
    for hidden, weight in zip(hiddens[1:], weights[1:]):
        total = total + dot(hidden[...], weight[...], 1, 0)
    out_ref[...] = (mid_ref[...] + total + b_ref[...]).astype(bf16)


def mid_back_kernel(count, *refs):
    mid_ref, gout_ref = refs[:2]
    dpres = refs[2 : 2 + count]
    gain_ref, shift_ref = refs[2 + count : 4 + count]
    weights = refs[4 + count : 4 + 2 * count]
    dmid_ref, dmid_b_ref, sums_ref = refs[4 + 2 * count :]

    @pl.when(pl.program_id(0) == 0)
    def _():
        sums_ref[...] = jnp.zeros_like(sums_ref)

    dxn = dot(dpres[0][...], weights[0][...], 1, 1)
    for dpre, weight in zip(dpres[1:], weights[1:]):
        dxn = dxn + dot(dpre[...], weight[...], 1, 1)
    gain = gain_ref[...]
    _, normed, scale_inv = norm_forward(mid_ref[...], gain, shift_ref[...])
    gout = gout_ref[...].astype(f32)
    dmid = gout + norm_backward(dxn, normed, scale_inv, gain)
    dmid_ref[...] = dmid
    dmid_b_ref[...] = dmid.astype(bf16)
    for at, value in enumerate((dxn * normed, dxn, dmid, gout)):
        sums_ref[at : at + 1, :] += jnp.sum(value, axis=0, keepdims=True)


def in_back_kernel(count, *refs):
    x_ref, dmid_ref = refs[:2]
    grads = refs[2 : 2 + count]
    gain_ref, shift_ref = refs[2 + count : 4 + count]
    weights = refs[4 + count : 4 + 2 * count]
    out_ref, sums_ref = refs[4 + 2 * count :]

    @pl.when(pl.program_id(0) == 0)
    def _():
        sums_ref[...] = jnp.zeros_like(sums_ref)

    dxn = jnp.zeros(dmid_ref.shape, f32)
    for at in range(count):
        for c in range(3):
            cols = weights[at].shape[2]
            dxn = dxn + dot(grads[at][:, c * cols : (c + 1) * cols], weights[at][c], 1, 1)
    gain = gain_ref[...]
    _, normed, scale_inv = norm_forward(x_ref[...].astype(f32), gain, shift_ref[...])
    out_ref[...] = (dmid_ref[...] + norm_backward(dxn, normed, scale_inv, gain)).astype(bf16)
    for at, value in enumerate((dxn * normed, dxn)):
        sums_ref[at : at + 1, :] += jnp.sum(value, axis=0, keepdims=True)


def local(
    inputs,
    image_count,
    rel_index,
    rel_table,
    norm1_gain,
    norm1_shift,
    w_qkv,
    bias_qv,
    w_proj,
    b_proj,
    norm2_gain,
    norm2_shift,
    w_fc1,
    b_fc1,
    w_fc2,
    b_fc2,
    out_grad,
):
    rows, width = inputs.shape
    window = rel_index.shape[0]
    offsets, heads = rel_table.shape
    shards = lax.axis_size(TENSOR)
    me = lax.axis_index(TENSOR)
    head_dim = w_qkv.shape[2] // heads
    scale = head_dim ** (-0.5)
    windows = rows // window
    padded = -(-window // ROW_TILE) * ROW_TILE
    n = windows * padded
    row = lambda value: value.reshape(1, -1)

    def swap(value, bit):
        return lax.ppermute(value, TENSOR, [(i, i ^ bit) for i in range(shards)])

    def gather(value):
        got = [value]
        for m in range(1, shards):
            low = m & -m
            got.append(swap(got[m ^ low], low))
        return got

    def cut_rows(value):
        return value.reshape(windows, padded, -1)[:, :window].reshape(rows, -1)

    index = jnp.pad(
        rel_index, ((0, padded - window), (0, padded - window)), constant_values=-1
    )
    onehot = (index[:, :, None] == jnp.arange(offsets, dtype=jnp.int32)).astype(f32)
    bias = jnp.einsum("qkt,th->khq", onehot, rel_table, precision=lax.Precision.HIGHEST)
    keys = jnp.arange(padded, dtype=jnp.int32)[:, None, None]
    bias = jnp.where(keys < window, bias, FAR_BELOW).reshape(padded, heads * padded)

    biases = gather(bias)
    vectors = gather(row(jnp.concatenate([bias_qv.reshape(-1), b_fc1])))
    wqs = gather(w_qkv)
    wps = gather(w_proj)
    w1s = gather(w_fc1)
    w2s = gather(w_fc2)

    live_rows = image_count[0] * IMG_TOKENS - me * rows
    live = (jnp.arange(rows, dtype=jnp.int32) < live_rows)[:, None]
    x_pad, xn1, gout = prepare(
        live_rows, inputs, out_grad, row(norm1_gain), row(norm1_shift), window, padded
    )

    order = range(shards)
    qkvs, probs, atts = [], [], []
    for m in order:
        qkv, p, att = attend(xn1, wqs[m], vectors[m], biases[m], heads, scale, windows, padded)
        qkvs.append(qkv)
        probs.append(p)
        atts.append(att.reshape(n, -1))

    mid, xn2 = by_rows(
        functools.partial(enter_kernel, shards),
        n,
        [from_hbm(v) for v in [x_pad] + atts],
        [row(b_proj), row(norm2_gain), row(norm2_shift)] + wps,
        [kept((n, width)), shape_of((n, width), bf16)],
        [],
        2 * n * width * width,
    )

    ff = w_fc1.shape[1]
    hiddens, dpres, g_b1s, g_fcs = {}, {}, {}, {}
    back_order = list(reversed(order))
    for m in mlp_order(shards):
        hiddens[m], dpres[m], g_b1s[m], g_fcs[m] = by_rows(
            functools.partial(mlp_kernel, bias_qv.size),
            n,
            [xn2, gout],
            [w1s[m], vectors[m], w2s[m]],
            [kept((n, ff), bf16), kept((n, ff), bf16)],
            [shape_of((1, ff)), shape_of((2 * ff, width), bf16)],
            8 * n * width * ff,
            [pltpu.VMEM((2 * ff, width), f32)],
            n,
        )

    def scatter(parts):
        held = {m: [parts[m]] for m in parts}
        for m in range(shards - 1, 0, -1):
            low = m & -m
            total = held[m][0]
            for term in held[m][1:]:
                total = total + term
            held[m ^ low].append(swap(total, low))
        return held[0]

    groups = lax.axis_size(DP)
    group = lax.axis_index(DP)

    def swap_dp(value, bits):
        return lax.ppermute(value, DP, [(i, i ^ bits) for i in range(groups)])

    def swap_all(pieces, stride):
        got = []
        for j, piece in enumerate(pieces):
            got.append(swap_dp(piece, j * stride) if j else piece)
        return got

    def sum_dp(terms, ways, results):
        stages = []
        stride = 1
        for way in ways:
            stages.append((stride, way, (group // stride % way).reshape(1)))
            stride *= way
        first = terms[0]
        for stride, way, digit in stages:
            pieces = split(terms, digit, way)
            first = pieces[0]
            terms = swap_all(pieces, stride)
        total = terms[0].astype(f32)
        for term in terms[1:]:
            total = total + term.astype(f32)
        total = total.astype(bf16)
        for at, (stride, way, digit) in reversed(list(enumerate(stages))):
            pieces = swap_all([total] * way, stride)
            total = merge(pieces, digit, None if at else results)
        return total, first

    def ways_of(most):
        left = groups
        ways = []
        while left > 1:
            ways.append(min(most[min(len(ways), len(most) - 1)], left))
            left //= ways[-1]
        return ways

    g_fc, _ = sum_dp(scatter(g_fcs), ways_of((4, 2)), [(width, ff), (ff, width)])
    g_fc1, g_fc2 = g_fc

    listed = lambda parts: [parts[m] for m in order]
    dmid, dmid_b, sums2 = by_rows(
        functools.partial(mid_back_kernel, shards),
        n,
        [from_hbm(v) for v in [mid, gout] + listed(dpres)],
        [row(norm2_gain), row(norm2_shift)] + w1s,
        [kept((n, width)), shape_of((n, width), bf16)],
        [shape_of((8, width))],
        2 * n * width * ff * shards,
    )

    dqkvs, dss, g_bqvs, g_atts = {}, {}, {}, {}
    for m in back_order:
        dqkv, g_atts[m], dss[m], g_bqvs[m] = attend_back(
            dmid_b, xn1, wps[m], qkvs[m], probs[m], atts[m], heads, scale
        )
        dqkvs[m] = dqkv.reshape(n, -1)
    g_att, after_split = sum_dp(scatter(g_atts), ways_of((4, 2)), [w_qkv.shape, w_proj.shape])
    g_qkv, g_proj = g_att

    in_grad, sums1 = by_rows(
        functools.partial(in_back_kernel, shards),
        n,
        [from_hbm(v) for v in [x_pad, dmid] + listed(dqkvs)],
        [row(norm1_gain), row(norm1_shift)] + wqs,
        [shape_of((n, width), bf16)],
        [shape_of((8, width))],
        6 * n * width * width,
        chunk=CHUNK // 2,
    )
    (outputs,) = by_rows(
        functools.partial(leave_kernel, shards),
        n,
        [from_hbm(v) for v in [mid] + listed(hiddens)],
        [row(b_fc2)] + w2s,
        [shape_of((n, width), bf16)],
        [],
        2 * n * width * ff * shards,
    )
    outputs = cut_rows(outputs)
    outputs = jnp.where(live, outputs, jnp.zeros_like(outputs))
    in_grad = cut_rows(in_grad)

    *late_ds, _ = lax.optimization_barrier((*listed(dss), after_split))
    ds_all = jnp.stack(late_ds).reshape(shards, padded, heads, padded)
    g_tabs = jnp.einsum(
        "qkt,mkhq->mth", onehot, ds_all, precision=lax.Precision.HIGHEST
    )
    per_shard = jnp.concatenate(
        [
            g_tabs.reshape(shards, -1),
            jnp.stack(listed(g_bqvs)).reshape(shards, -1),
            jnp.stack(listed(g_b1s)).reshape(shards, -1),
        ],
        axis=1,
    )
    shared = jnp.concatenate([sums2[:4].reshape(-1), sums1[:2].reshape(-1)])
    per_shard = jnp.concatenate(
        [per_shard, jnp.broadcast_to(shared, (shards, shared.size))], axis=1
    )
    small = per_shard[0]
    for m in range(1, shards):
        small = small + swap(per_shard[m], m)
    stride = 1
    for at, way in enumerate(ways_of((4, 2))):
        small = sum(swap_all([small] * way, stride))
        stride *= way
    pieces = []
    at = 0
    for shape in (rel_table.shape, bias_qv.shape, b_fc1.shape) + ((width,),) * 6:
        size = 1
        for extent in shape:
            size *= extent
        pieces.append(small[at : at + size].reshape(shape))
        at += size
    g_tab, g_bqv, g_b_fc1, g_n2g, g_n2s, g_bp, g_b_fc2, g_n1g, g_n1s = pieces
    return (
        outputs,
        in_grad,
        g_tab,
        g_n1g,
        g_n1s,
        g_qkv,
        g_bqv,
        g_proj,
        g_bp,
        g_n2g,
        g_n2s,
        g_fc1,
        g_b_fc1,
        g_fc2,
        g_b_fc2,
    )


def mlp_order(shards):
    return [1] * (shards > 1) + [m for m in range(shards - 1, -1, -1) if m != 1]


def solution(mesh):
    placed = (
        P((DP, TENSOR), None),
        P(DP),
        P(),
        P(None, TENSOR),
        P(),
        P(),
        P(None, None, TENSOR),
        P(None, TENSOR),
        P(TENSOR, None),
        P(),
        P(),
        P(),
        P(None, TENSOR),
        P(TENSOR),
        P(TENSOR, None),
        P(),
        P((DP, TENSOR), None),
    )
    return jax.shard_map(
        local,
        mesh=mesh,
        in_specs=placed,
        out_specs=(
            P((DP, TENSOR), None),
            P((DP, TENSOR), None),
            P(None, TENSOR),
            P(),
            P(),
            P(None, None, TENSOR),
            P(None, TENSOR),
            P(TENSOR, None),
            P(),
            P(),
            P(),
            P(None, TENSOR),
            P(TENSOR),
            P(TENSOR, None),
            P(),
        ),
        check_vma=False,
    )
```
